32 devices in a mesh: rep: 2 (over core), exp: 16 (over z, y, x).
Axes of the slice: x: 2, y: 2, z: 4, core: 2. Of those that a mesh axis runs over, the one named last changes fastest.
Arguments:
- tokens: bfloat16 [4096, 4096], P(('rep', 'exp')), may hold values from -6 to 6
- expert_ids: int32 [4096, 8], P(('rep', 'exp')), may hold values from 0 to 15, all different within a row; in each aligned block of 128 rows (0 to 127, 128 to 255, ...) at most 72 rows name the same one
- route_weights: bfloat16 [4096, 8], P(('rep', 'exp')), may hold values from 0.099609375 to 1
- cotangent: bfloat16 [4096, 4096], P(('rep', 'exp')), may hold values from -0.3984375 to 0.3984375
- w_gate: bfloat16 [16, 4096, 768], P('exp'), may hold values from -0.09375 to 0.09375
- w_up: bfloat16 [16, 4096, 768], P('exp'), may hold values from -0.09375 to 0.09375
- w_down: bfloat16 [16, 768, 4096], P('exp'), may hold values from -0.21875 to 0.21875
- ia3_scale: float32 [16, 768], P('exp'), may hold values from 0.25 to 1.75
Outputs:
- mixed: bfloat16 [4096, 4096], P(('rep', 'exp'))
- ia3_grad: float32 [16, 768], P('exp')
The draws below stay inside these ranges and needn't reach their ends.
Inputs may be any that keep to these rules, and one draw needn't show every extreme that they name: `expert_ids`: among the choices of one device's 128 tokens, no expert is named more than 72 times, a bound that some block reaches; a token names 8 different experts.
All inputs are finite; a program needn't handle non-finite values.
Results may differ from the reference program's by a relative error of at most 0.0057.
Values may be sent and summed in bfloat16 or wider, within the bound.
No kernel may reach another device: no remote copies, remote signals or barrier semaphores. Data moves between devices by JAX's collectives and lax.ppermute only.
A program may use at most 192 MiB of HBM per device.

```python
import math
import jax
import jax.numpy as jnp
import numpy as np
from jax import lax

D = 4096
FF = 768
TOP = 8
TOK_DEV = 128
EXPERTS = 16
TOKENS = 4096
MOST = 72


def steps_of(key, shape, pieces, low, high):
    def one(position, blocks):
        steps = jax.random.uniform(jax.random.fold_in(jax.random.fold_in(key, 6), position), (blocks,), jnp.float32, low / len(pieces), high / len(pieces))
        return jnp.repeat(jnp.exp(steps), shape[position] // blocks).reshape((-1,) + (1,) * (len(shape) - position - 1))

    loudness = one(*pieces[0])
    for cut in pieces[1:]:
        loudness = loudness * one(*cut)
    return loudness


def shared_out(rng, own, number, rows, number_of, top, most, skew):
    ranking = jax.random.permutation(rng, number_of)
    packed, ordinary = load_shares(number_of, rows * top, most, skew, True), load_shares(number_of, rows * top, most, skew, False)
    places = jnp.arange(number_of)

    def named(lengths, rotation):
        used = int((lengths > 0).sum())
        fixed = max(1, used // 4)
        shifted = fixed + (places - fixed + rotation * (used - fixed)) % max(1, number_of - fixed)
        return jnp.zeros((number_of,), jnp.int32).at[ranking[jnp.where(places < fixed, places, shifted)]].set(jnp.asarray(lengths, jnp.int32))

    lengths = jnp.where(number % 4 == 0, named(packed, number // 4), named(ordinary, number - number // 4 - 1))
    mixed = jax.random.permutation(jax.random.fold_in(own, 3), number_of)
    giver, sink = mixed[0:number_of // 2 * 2:2], mixed[1:number_of // 2 * 2:2]
    margin = jnp.minimum(lengths[giver] - 1, most - lengths[sink]) // 2
    margin = jnp.where((giver == ranking[0]) | (sink == ranking[0]) | (lengths[sink] == 0), 0, jnp.maximum(margin, 0))
    shifted = jax.random.randint(jax.random.fold_in(own, 4), (number_of // 2,), 0, 1 << 20) % (margin + 1)
    lengths = lengths.at[giver].add(-shifted).at[sink].add(shifted)
    items = jnp.searchsorted(jnp.cumsum(lengths), jnp.arange(rows * top), side="right").astype(jnp.int32)
    grid = items.reshape(top, rows).T
    grid = grid[jax.random.permutation(jax.random.fold_in(own, 1), rows)]
    rotation = jax.random.randint(jax.random.fold_in(own, 2), (rows, 1), 0, top)
    return jnp.take_along_axis(grid, (jnp.arange(top)[None, :] + rotation) % top, axis=1)


def load_shares(amount, total, limit, slope, full):
    loads = [(1 << 20) // math.isqrt(rank ** slope) + 1 for rank in range(1, amount + 1)]
    largest = limit if full else min(limit, max(-(-total // amount), total * loads[0] // sum(loads)))
    least = 1 if total - largest >= amount - 1 else 0
    holding, surplus = [largest] + [least] * (amount - 1), total - largest - least * (amount - 1)
    while surplus > 0:
        candidates = [i for i in range(1, amount) if holding[i] < largest] or [i for i in range(1, amount) if holding[i] < limit]
        mass, left = sum([loads[i] for i in candidates]), surplus
        for i in candidates:
            extra = min(limit - holding[i], max(1, left * loads[i] // mass), surplus)
            holding[i] = holding[i] + extra
            surplus = surplus - extra
    return np.array(holding)


def normal_values(key, dims, scale, bound, cuts=(), kind=jnp.bfloat16):
    entries = scale * jax.random.normal(key, dims, jnp.float32)
    if cuts:
        entries = entries * steps_of(key, dims, cuts, -0.22, 0.18)
    return jnp.clip(entries, -bound, bound).astype(kind)


def setup_inputs(seed: int = 0) -> dict:
    key_list = jax.random.split(jax.random.key(seed), 9)
    tokens = normal_values(key_list[0], (TOKENS, D), 1.0, 6.0, ((0, 32),))
    expert_ids_keys = jax.random.split(jax.random.fold_in(key_list[1], 1), TOKENS // TOK_DEV)
    expert_ids_turns = jax.random.permutation(jax.random.fold_in(key_list[1], 3), TOKENS // TOK_DEV)
    expert_ids = jax.vmap(lambda own, number: shared_out(jax.random.fold_in(key_list[1], 2), own, number, TOK_DEV, EXPERTS, TOP, MOST, 1))(expert_ids_keys, expert_ids_turns).reshape((TOKENS, TOP))
    route_weights = jnp.clip(0.099609375 + 0.9003906 * jax.random.uniform(key_list[2], (TOKENS, TOP), jnp.float32) ** steps_of(key_list[2], (TOKENS, TOP), ((0, 32),), -0.2, 0.2), 0.099609375, 1.0).astype(jnp.bfloat16)
    cotangent = normal_values(key_list[3], (TOKENS, D), 0.05, 0.3984375, ((0, 32),))
    w_gate = normal_values(key_list[4], (EXPERTS, D, FF), D ** -0.5, 0.09375, ((0, 16),))
    w_up = normal_values(key_list[5], (EXPERTS, D, FF), D ** -0.5, 0.09375, ((0, 16),))
    w_down = normal_values(key_list[6], (EXPERTS, FF, D), FF ** -0.5, 0.21875, ((0, 16),))
    ia3_scale = jnp.clip(1.0 + 0.15 * jax.random.normal(key_list[7], (EXPERTS, FF), jnp.float32), 0.25, 1.75)
    return dict(tokens=tokens, expert_ids=expert_ids, route_weights=route_weights, cotangent=cotangent, w_gate=w_gate, w_up=w_up, w_down=w_down, ia3_scale=ia3_scale)


def reference(tokens, expert_ids, route_weights, cotangent, w_gate, w_up, w_down, ia3_scale):
    flat_ids = expert_ids.reshape(-1)
    flat_weights = route_weights.reshape(-1).astype(jnp.float32)
    capacity = (TOKENS // TOK_DEV) * MOST

    def per_expert(y_total, expert):
        matches = flat_ids == expert
        (chosen,) = jnp.nonzero(matches, size=capacity, fill_value=0)
        chosen = chosen.astype(jnp.int32)
        used_count = jnp.sum(matches.astype(jnp.int32))
        is_valid = (jnp.arange(capacity, dtype=jnp.int32) < used_count).astype(jnp.float32)
        token_index = (chosen // TOP).astype(jnp.int32)
        gathered = tokens[token_index]
        weight_row = flat_weights[chosen] * is_valid
        gate_pre = jnp.dot(gathered, w_gate[expert], preferred_element_type=jnp.float32)
        up_pre = jnp.dot(gathered, w_up[expert], preferred_element_type=jnp.float32)
        activated = jax.nn.silu(gate_pre) * up_pre
        hidden = (ia3_scale[expert][None, :] * activated).astype(jnp.bfloat16)
        expert_out = jnp.dot(hidden, w_down[expert], preferred_element_type=jnp.float32).astype(jnp.bfloat16)
        y_total = y_total.at[token_index].add(weight_row[:, None] * expert_out.astype(jnp.float32))
        back_proj = lax.dot_general(cotangent[token_index], w_down[expert], (((1,), (1,)), ((), ())), preferred_element_type=jnp.float32)
        grad_row = jnp.sum(weight_row[:, None] * activated * back_proj, axis=0)
        return y_total, grad_row

    start = jnp.zeros((TOKENS, D), jnp.float32)
    y_total, grads = lax.scan(per_expert, start, jnp.arange(EXPERTS, dtype=jnp.int32))
    return y_total.astype(jnp.bfloat16), grads
```

```python
import jax
import jax.numpy as jnp
from jax import lax
from jax.sharding import PartitionSpec as P

PIECES = 2
CHUNKS = 4
F32 = jnp.float32
BF16 = jnp.bfloat16


def ring_order(members):
    return list(range(0, members, 2)) + list(reversed(range(1, members, 2)))


def ring_perm(members, step):
    order = ring_order(members)
    perm = []
    for parity in range(2):
        for place, member in enumerate(order):
            target = order[(place + step) % members]
            perm.append((2 * member + parity, 2 * target + parity))
    return perm


def dot(a, b):
    return jnp.dot(a, b, preferred_element_type=F32)


def dot_t(a, b):
    return lax.dot_general(a, b, (((1,), (1,)), ((), ())), preferred_element_type=F32)


def gathered(tokens, expert_ids, route_weights, cotangent, w_gate, w_up, w_down, ia3_scale):
    owners = lax.axis_size("exp")
    members = owners // 2
    rows, width = tokens.shape
    hidden_units = w_gate.shape[2]
    half_units = hidden_units // 2
    me = lax.axis_index("exp")
    rep = lax.axis_index("rep")
    w_gate, w_up, w_down = w_gate[0], w_up[0], w_down[0]
    forward, backward = ring_perm(members, 1), ring_perm(members, -1)
    pair = [(i, i ^ 1) for i in range(owners)]
    cores = [(0, 1), (1, 0)]
    full = (members - 1) // 2
    opposite = members % 2 == 0
    split = rows // 2

    def go(value, perm):
        return lax.ppermute(value, "exp", perm)

    def from_pair(value):
        mine = go(value, pair)
        return mine, lax.ppermute(mine, "rep", cores)

    def gather(block):
        ahead = behind = block
        blocks = [block]
        for _ in range(full):
            ahead, behind = go(ahead, forward), go(behind, backward)
            blocks += [ahead, behind]
        if opposite:
            blocks += [go(ahead[:split], forward), go(behind[split:], backward)]
        return jnp.concatenate(blocks)

    depth = width // PIECES
    first = rep * half_units
    projections = []
    for piece in range(PIECES):
        top = piece * depth
        cut = [
            lax.dynamic_slice(w, (top, first), (depth, half_units)) for w in (w_gate, w_up)
        ]
        projections.append(from_pair(jnp.concatenate(cut, axis=1)))
    columns = width // CHUNKS
    downs = []
    for chunk in range(CHUNKS):
        cut = lax.dynamic_slice(w_down, (first, chunk * columns), (half_units, columns))
        downs.append(jnp.concatenate(from_pair(cut), axis=0))

    named = expert_ids[:, :, None] == jnp.arange(owners, dtype=jnp.int32)
    table = jnp.sum(jnp.where(named, route_weights[:, :, None], 0).astype(F32), axis=1).astype(BF16)
    table = table.T

    def spread(block):
        blocks = [block]
        for step in range(1, full + 1):
            blocks += [go(block, ring_perm(members, step)), go(block, ring_perm(members, -step))]
        if opposite:
            blocks.append(go(block, ring_perm(members, members // 2)))
        return jnp.concatenate(blocks, axis=1)

    tables = spread(table)
    weight_own = lax.dynamic_slice(tables, (me, 0), (1, tables.shape[1])).astype(F32).reshape(-1, 1)
    weight_pair = lax.dynamic_slice(tables, (me ^ 1, 0), (1, tables.shape[1])).astype(F32).reshape(-1, 1)

    scale_own = ia3_scale
    scale_pair_mine, scale_pair_other = from_pair(lax.dynamic_slice(ia3_scale, (0, first), (1, half_units)))

    all_tokens = gather(tokens)
    all_cotangents = gather(cotangent)

    act_own = jax.nn.silu(dot(all_tokens, w_gate)) * dot(all_tokens, w_up)
    hidden_own = (scale_own * act_own).astype(BF16)
    part_own = weight_own * dot(hidden_own, w_down)

    acts, hiddens = [], []
    for side, scale in enumerate((scale_pair_mine, scale_pair_other)):
        pre = sum(
            dot(all_tokens[:, piece * depth : (piece + 1) * depth], projections[piece][side])
            for piece in range(PIECES)
        )
        act = jax.nn.silu(pre[:, :half_units]) * pre[:, half_units:]
        acts.append(act)
        hiddens.append((scale * act).astype(BF16))
    hidden_pair = jnp.concatenate(hiddens, axis=1)

    def scatter_sum(part):
        def block(index):
            return part[index * rows : (index + 1) * rows]

        ahead = behind = None
        if opposite:
            last = block(2 * full + 1)
            ahead, behind = go(last[split:].astype(BF16), forward), go(last[:split].astype(BF16), backward)
        for step in range(full, 0, -1):
            toward, back = block(2 * step), block(2 * step - 1)
            if ahead is not None:
                if step == full:
                    toward = jnp.concatenate([toward[:split], toward[split:] + ahead.astype(F32)])
                    back = jnp.concatenate([back[:split] + behind.astype(F32), back[split:]])
                else:
                    toward, back = toward + ahead.astype(F32), back + behind.astype(F32)
            ahead, behind = go(toward.astype(BF16), forward), go(back.astype(BF16), backward)
        own = block(0)
        if full == 0:
            return (own + jnp.concatenate([behind, ahead]).astype(F32)).astype(BF16)
        return (own + ahead.astype(F32) + behind.astype(F32)).astype(BF16)

    mixed = []
    for chunk in range(CHUNKS):
        part = part_own[:, chunk * columns : (chunk + 1) * columns]
        part = part + weight_pair * dot(hidden_pair, downs[chunk])
        mixed.append(scatter_sum(part))
    mixed = jnp.concatenate(mixed, axis=1)

    back_own = dot_t(all_cotangents, w_down)
    grad_own = jnp.sum(weight_own * act_own * back_own, axis=0)
    back_pair = sum(
        dot_t(all_cotangents[:, chunk * columns : (chunk + 1) * columns], downs[chunk])
        for chunk in range(CHUNKS)
    )
    act_pair = jnp.concatenate(acts, axis=1)
    grad_pair = jnp.sum(weight_pair * act_pair * back_pair, axis=0)
    mine, other = grad_pair[:half_units], grad_pair[half_units:]
    grad_pair = jnp.where(rep == 0, jnp.concatenate([mine, other]), jnp.concatenate([other, mine]))
    total = (grad_own + go(grad_pair, pair))[None, :]
    total = total + lax.ppermute(total, "rep", cores)
    return mixed, total


def exchanged(tokens, expert_ids, route_weights, cotangent, w_gate, w_up, w_down, ia3_scale):
    owners = lax.axis_size("exp")
    tok_rows, model_width = tokens.shape
    per_token = expert_ids.shape[1]
    capacity = tok_rows * per_token // owners + tok_rows * per_token // (8 * owners)
    flat_ids = expert_ids.reshape(-1)
    one_hot = (flat_ids[:, None] == jnp.arange(owners, dtype=jnp.int32)[None, :]).astype(jnp.int32)
    before = jnp.cumsum(one_hot, axis=0) - one_hot
    slot_index = jnp.sum(before * one_hot, axis=1)
    source_row = jnp.arange(tok_rows * per_token, dtype=jnp.int32) // per_token

    def into_slots(values):
        empty = jnp.zeros((owners, capacity) + values.shape[1:], values.dtype)
        return empty.at[flat_ids, slot_index].set(values)

    token_send = into_slots(tokens[source_row])
    weight_send = into_slots(route_weights.reshape(-1))
    token_recv, weight_recv = (
        lax.all_to_all(token_send, "exp", split_axis=0, concat_axis=0, tiled=True),
        lax.all_to_all(weight_send, "exp", split_axis=0, concat_axis=0, tiled=True),
    )
    received_rows = token_recv.reshape(-1, model_width)
    gate_pre = jnp.dot(received_rows, w_gate[0], preferred_element_type=jnp.float32)
    up_pre = jnp.dot(received_rows, w_up[0], preferred_element_type=jnp.float32)
    activated = jax.nn.silu(gate_pre) * up_pre
    hidden = (ia3_scale[0][None, :] * activated).astype(jnp.bfloat16)
    expert_out = jnp.dot(hidden, w_down[0], preferred_element_type=jnp.float32).astype(jnp.bfloat16)
    returned = lax.all_to_all(
        expert_out.reshape(owners, capacity, model_width),
        "exp",
        split_axis=0,
        concat_axis=0,
        tiled=True,
    )
    picked = returned[flat_ids, slot_index].reshape(tok_rows, per_token, model_width)
    mixed = jnp.einsum(
        "tkd,tk->td", picked, route_weights, preferred_element_type=jnp.float32
    ).astype(jnp.bfloat16)
    grad_send = into_slots(cotangent[source_row])
    grad_recv = lax.all_to_all(grad_send, "exp", split_axis=0, concat_axis=0, tiled=True)
    back_proj = lax.dot_general(
        grad_recv.reshape(-1, model_width),
        w_down[0],
        (((1,), (1,)), ((), ())),
        preferred_element_type=jnp.float32,
    )
    weight_rows = weight_recv.reshape(-1).astype(jnp.float32)
    local_grad = jnp.sum(weight_rows[:, None] * activated * back_proj, axis=0)
    summed = lax.psum(local_grad, "rep")
    return (mixed, summed[None, :])


def shards(*arrays):
    owners = lax.axis_size("exp")
    dense = owners % 2 == 0 and owners > 2 and 2 * arrays[1].shape[1] >= owners
    return gathered(*arrays) if dense else exchanged(*arrays)


def solution(mesh):
    in_specs = (
        P(("rep", "exp"), None),
        P(("rep", "exp"), None),
        P(("rep", "exp"), None),
        P(("rep", "exp"), None),
        P("exp", None, None),
        P("exp", None, None),
        P("exp", None, None),
        P("exp", None),
    )
    out_specs = (P(("rep", "exp"), None), P("exp", None))
    return jax.shard_map(shards, mesh=mesh, in_specs=in_specs, out_specs=out_specs, check_vma=False)
```

```python
import functools
import math

import jax
import jax.numpy as jnp
from jax import lax
from jax.experimental import pallas as pl
from jax.experimental.pallas import tpu as pltpu
from jax.sharding import PartitionSpec as P

PIECES = (2, 1)
SHARES = (3, 3, 2)
SLOTS = 3
LANES = 128
EARLY = 2
F32 = jnp.float32
BF16 = jnp.bfloat16
VMEM_LIMIT = 60 * 1024 * 1024


def ring_order(members):
    return list(range(0, members, 2)) + list(reversed(range(1, members, 2)))


def ring_perm(members, step):
    order = ring_order(members)
    perm = []
    for parity in range(2):
        for place, member in enumerate(order):
            target = order[(place + step) % members]
            perm.append((2 * member + parity, 2 * target + parity))
    return perm


def bounds_of(width, shares):
    edges = [0]
    for share in shares:
        edges.append(edges[-1] + width * share // sum(shares))
    return list(zip(edges[:-1], edges[1:]))


def whole(shape):
    return pl.BlockSpec(shape, lambda *_: (0,) * len(shape))


def params():
    return pltpu.CompilerParams(vmem_limit_bytes=VMEM_LIMIT)


def cost(flops, *arrays):
    moved = sum(math.prod(a.shape) * a.dtype.itemsize for a in arrays)
    return pl.CostEstimate(flops=flops, transcendentals=0, bytes_accessed=moved)


def cut_columns(core, w_gate, w_up, low, high):
    depth, units = w_gate.shape
    per_half, tiles = units // 2 // LANES, (high - low) // LANES
    step = math.gcd(depth, 1024)

    def body(core_ref, *refs):
        out_ref = refs[-1]
        for n, ref in enumerate(refs[:-1]):
            out_ref[:, n * LANES : (n + 1) * LANES] = ref[...]

    specs = [
        pl.BlockSpec((step, LANES), lambda i, core_ref, n=n: (i, core_ref[0] * per_half + low // LANES + n))
        for n in range(tiles)
    ]
    out = jax.ShapeDtypeStruct((depth, 2 * (high - low)), w_gate.dtype)
    return pl.pallas_call(
        body,
        out_shape=out,
        grid_spec=pltpu.PrefetchScalarGridSpec(
            num_scalar_prefetch=1,
            grid=(depth // step,),
            in_specs=specs + specs,
            out_specs=pl.BlockSpec((step, 2 * (high - low)), lambda i, core_ref: (i, 0)),
        ),
        cost_estimate=cost(0, out, out),
        name="cut_columns",
    )(core, *[w_gate] * tiles, *[w_up] * tiles)


def cut_rows(core, w_down, bounds):
    half, width = w_down.shape[0] // 2, w_down.shape[1]
    step = half // 3 if half % 48 == 0 else half

    def body(core_ref, in_ref, *out_refs):
        for (low, high), out_ref in zip(bounds, out_refs):
            out_ref[...] = in_ref[:, low:high]

    outs = [jax.ShapeDtypeStruct((half, high - low), w_down.dtype) for low, high in bounds]
    return pl.pallas_call(
        body,
        out_shape=outs,
        grid_spec=pltpu.PrefetchScalarGridSpec(
            num_scalar_prefetch=1,
            grid=(half // step,),
            in_specs=[pl.BlockSpec((step, width), lambda i, core_ref: (core_ref[0] * (half // step) + i, 0))],
            out_specs=[pl.BlockSpec((step, high - low), lambda i, core_ref: (i, 0)) for low, high in bounds],
        ),
        cost_estimate=cost(0, *outs, *outs),
        name="cut_rows",
    )(core, w_down)


def contract(blocks, groups, transposed, extras, outs, finish):
    starts = [0]
    for block in blocks:
        starts.append(starts[-1] + block.shape[0])
    rows, width = starts[-1], blocks[0].shape[1]
    step = math.gcd(512, width)
    arrays, copies_of, sizes = [], [], []
    for parts in groups:
        size = 0
        for segments, take, place in parts:
            at = 0
            for array, length in segments:
                if not any(array is other for other in arrays):
                    arrays.append(array)
                index = next(i for i, other in enumerate(arrays) if other is array)
                assert length % step == 0
                copies_of.append((len(sizes), index, at // step, length // step, take, place))
                at += length
            size = max(size, place + take.stop - take.start)
        sizes.append(size)
    steps = width // step
    count, parts_count = len(blocks), len(copies_of)
    slots = min(SLOTS, steps)

    def body(*refs):
        block_refs, refs = refs[:count], refs[count:]
        array_refs, refs = refs[: len(arrays)], refs[len(arrays) :]
        extra_refs, refs = refs[: len(extras)], refs[len(extras) :]
        out_refs, refs = refs[: len(outs)], refs[len(outs) :]
        held, sems, weight_sems, refs = refs[0], refs[1], refs[2], refs[3:]
        weight_refs, totals = refs[: len(sizes)], refs[len(sizes) :]
        k = pl.program_id(0)

        def block_copies(at, slot):
            columns = pl.ds(pl.multiple_of(at * step, step), step)
            return [
                pltpu.make_async_copy(
                    ref.at[:, columns],
                    held.at[slot, pl.ds(starts[i], blocks[i].shape[0]), :],
                    sems.at[slot, i],
                )
                for i, ref in enumerate(block_refs)
            ]

        def weight_copy(part, at, slot):
            j, index, first, _, take, place = copies_of[part]
            along = pl.ds(pl.multiple_of((at - first) * step, step), step)
            across = pl.ds(take.start, take.stop - take.start)
            there = pl.ds(place, take.stop - take.start)
            if transposed:
                source, target = array_refs[index].at[across, along], weight_refs[j].at[slot, there, :]
            else:
                source, target = array_refs[index].at[along, across], weight_refs[j].at[slot, :, there]
            return pltpu.make_async_copy(source, target, weight_sems.at[slot, part])

        def each(at, slot, do):
            for copy in block_copies(at, slot):
                do(copy)
            for part, (_, _, first, length, _, _) in enumerate(copies_of):
                if length == steps:
                    do(weight_copy(part, at, slot))
                else:

                    @pl.when((at >= first) & (at < first + length))
                    def _():
                        do(weight_copy(part, at, slot))

        slot = lax.rem(k, slots)

        @pl.when(k == 0)
        def _():
            for early in range(slots - 1):
                each(early, early, lambda copy: copy.start())

        @pl.when(k + slots - 1 < steps)
        def _():
            each(k + slots - 1, lax.rem(k + slots - 1, slots), lambda copy: copy.start())

        each(k, slot, lambda copy: copy.wait())
        dims = (((1,), (1 if transposed else 0,)), ((), ()))

        def product(j):
            return lax.dot_general(held[slot], weight_refs[j][slot], dims, preferred_element_type=F32)

        @pl.when(k == 0)
        def _():
            for j, total in enumerate(totals):
                total[...] = product(j)

        @pl.when(k > 0)
        def _():
            for j, total in enumerate(totals):
                total[...] += product(j)

        @pl.when(k == steps - 1)
        def _():
            finish(totals, extra_refs, out_refs)

    specs = [pl.BlockSpec(memory_space=pl.ANY)] * (count + len(arrays))
    specs += [pl.BlockSpec(a.shape, lambda k: (0, 0), pipeline_mode=pl.Buffered(1)) for a in extras]
    dtype = blocks[0].dtype
    return pl.pallas_call(
        body,
        out_shape=outs,
        grid=(steps,),
        in_specs=specs,
        out_specs=[whole(out.shape) for out in outs],
        scratch_shapes=[
            pltpu.VMEM((slots, rows, step), dtype),
            pltpu.SemaphoreType.DMA((slots, count)),
            pltpu.SemaphoreType.DMA((slots, parts_count)),
            *[pltpu.VMEM((slots, size, step) if transposed else (slots, step, size), dtype) for size in sizes],
            *[pltpu.VMEM((rows, size), F32) for size in sizes],
        ],
        compiler_params=params(),
        cost_estimate=cost(2 * rows * sum(sizes) * width, *outs),
    )(*blocks, *arrays, *extras)


def silu(v):
    return v / (1.0 + jnp.exp(-v))


def finish_own(totals, extra_refs, out_refs):
    act = silu(totals[0][...]) * totals[1][...]
    out_refs[0][...] = (extra_refs[0][...] * act).astype(BF16)


def finish_pair(totals, extra_refs, out_refs):
    total = totals[0]
    size = total.shape[1] // 4
    for side in range(2):
        gate, up = total[:, 2 * side * size : (2 * side + 1) * size], total[:, (2 * side + 1) * size : (2 * side + 2) * size]
        columns = slice(side * size, (side + 1) * size)
        out_refs[0][:, columns] = (extra_refs[0][:, columns] * (silu(gate) * up)).astype(BF16)


def finish_grad(span, totals, extra_refs, out_refs):
    weight, scale, hiddens = extra_refs[0], extra_refs[1], extra_refs[2:]
    first = 0
    for hidden in hiddens:
        columns = slice(first, first + hidden.shape[1])
        term = weight[...] * hidden[span, :].astype(F32) * totals[0][:, columns]
        out_refs[0][:, columns] = jnp.sum(term, axis=0, keepdims=True) / scale[:, columns]
        first += hidden.shape[1]


def both_out(owns, pairs, takes, w_down, mine, other, weights, low, split):
    rows = sum(own.shape[0] for own in owns)
    units = w_down.shape[0]
    width = mine.shape[1]
    step = math.gcd(math.gcd(low, width), 512)

    def body(*refs):
        own_refs, refs = refs[: len(owns)], refs[len(owns) :]
        pair_refs, refs = refs[: len(pairs)], refs[len(pairs) :]
        w_ref, mine_ref, other_ref, weight_own, weight_pair, out_ref, near_ref, far_ref, hidden = refs

        @pl.when(pl.program_id(0) == 0)
        def _():
            done = 0
            for ref in own_refs:
                hidden[0, done : done + ref.shape[0], :] = ref[...]
                done += ref.shape[0]
            done = 0
            for ref in pair_refs:
                hidden[1, :, done : done + ref.shape[1]] = ref[...]
                done += ref.shape[1]

        w = jnp.concatenate([ref[take, :] for take in takes for ref in (mine_ref, other_ref)], axis=0)
        total = weight_own[...] * jnp.dot(hidden[0], w_ref[...], preferred_element_type=F32)
        total += weight_pair[...] * jnp.dot(hidden[1], w, preferred_element_type=F32)
        total = total.astype(BF16)
        out_ref[...] = total
        near_ref[...] = total[-2 * split : -split]
        far_ref[...] = total[-split:]

    def columns(height, first=0):
        return pl.BlockSpec((height, step), lambda j: (0, first // step + j))

    def fixed(a):
        return pl.BlockSpec(a.shape, lambda j: (0, 0), pipeline_mode=pl.Buffered(1))

    outs = [jax.ShapeDtypeStruct((height, width), BF16) for height in (rows, split, split)]
    return pl.pallas_call(
        body,
        out_shape=outs,
        grid=(width // step,),
        in_specs=[fixed(a) for a in (*owns, *pairs)]
        + [columns(units, low), columns(mine.shape[0]), columns(mine.shape[0])]
        + [fixed(a) for a in weights],
        out_specs=[columns(rows), columns(split), columns(split)],
        scratch_shapes=[pltpu.VMEM((2, rows, units), BF16)],
        compiler_params=params(),
        cost_estimate=cost(4 * rows * units * width, *outs),
    )(*owns, *pairs, w_down, mine, other, *weights)


def hop_sum(total, step, rows, ahead, behind):
    width = total.shape[1]
    split = ahead.shape[0]

    def body(toward_ref, back_ref, ahead_ref, behind_ref, out_toward, out_back):
        if split == rows:
            out_toward[...] = (toward_ref[...].astype(F32) + ahead_ref[...].astype(F32)).astype(BF16)
            out_back[...] = (back_ref[...].astype(F32) + behind_ref[...].astype(F32)).astype(BF16)
        else:
            out_toward[:split, :] = toward_ref[:split, :]
            out_toward[split:, :] = (toward_ref[split:, :].astype(F32) + ahead_ref[...].astype(F32)).astype(BF16)
            out_back[:split, :] = (back_ref[:split, :].astype(F32) + behind_ref[...].astype(F32)).astype(BF16)
            out_back[split:, :] = back_ref[split:, :]

    out = jax.ShapeDtypeStruct((rows, width), BF16)
    return pl.pallas_call(
        body,
        out_shape=[out, out],
        grid=(1,),
        in_specs=[
            pl.BlockSpec((rows, width), lambda i: (2 * step, 0)),
            pl.BlockSpec((rows, width), lambda i: (2 * step - 1, 0)),
            whole(ahead.shape),
            whole(behind.shape),
        ],
        out_specs=[whole(out.shape)] * 2,
        compiler_params=params(),
        cost_estimate=cost(0, out, out, out, out),
    )(total, total, ahead, behind)


def last_sum(chunks, rows, bounds):
    flat = [a for chunk in chunks for a in chunk]

    def body(*refs):
        out_ref = refs[-1]
        for n, (low, high) in enumerate(bounds):
            own, ahead, behind = refs[3 * n : 3 * n + 3]
            total = own[...].astype(F32) + ahead[...].astype(F32) + behind[...].astype(F32)
            out_ref[:, low:high] = total.astype(BF16)

    out = jax.ShapeDtypeStruct((rows, bounds[-1][1]), BF16)
    return pl.pallas_call(
        body,
        out_shape=out,
        grid=(1,),
        in_specs=[pl.BlockSpec((rows, a.shape[1]), lambda i: (0, 0)) for a in flat],
        out_specs=whole(out.shape),
        compiler_params=params(),
        cost_estimate=cost(0, out, out, out, out),
    )(*flat)


def gathered(tokens, expert_ids, route_weights, cotangent, w_gate, w_up, w_down, ia3_scale):
    owners = lax.axis_size("exp")
    members = owners // 2
    rows, width = tokens.shape
    units = w_gate.shape[2]
    half_units = units // 2
    me = lax.axis_index("exp")
    rep = lax.axis_index("rep")
    w_gate, w_up, w_down = w_gate[0], w_up[0], w_down[0]
    forward, backward = ring_perm(members, 1), ring_perm(members, -1)
    pair = [(i, i ^ 1) for i in range(owners)]
    cores = [(0, 1), (1, 0)]
    full = members // 2 - 1
    split = rows // 2

    def go(value, perm):
        return lax.ppermute(value, "exp", perm)

    def swap(value):
        return lax.ppermute(value, "rep", cores)

    def gather(block):
        halves = (block[:split], block[split:])
        ahead, behind = list(halves), list(halves)
        blocks = [block]
        for _ in range(1, full + 1):
            ahead = [go(ahead[h], forward) for h in range(2)]
            behind = [go(behind[h], backward) for h in range(2)]
            blocks += ahead + behind
        blocks.append(go(ahead[0], forward))
        blocks.append(go(behind[1], backward))
        return blocks

    pieces = bounds_of(half_units, PIECES)
    first = rep * half_units
    core = jnp.full((1,), rep, jnp.int32)
    projections = []
    for low, high in pieces:
        cut = cut_columns(core, w_gate, w_up, low, high)
        mine = go(cut, pair)
        projections.append((mine, swap(mine)))
    bounds = bounds_of(width, SHARES)
    cuts = cut_rows(core, w_down, bounds)
    downs = []
    for cut in cuts:
        mine = go(cut, pair)
        downs.append((mine, swap(mine)))

    named = expert_ids[:, :, None] == jnp.arange(owners, dtype=jnp.int32)
    table = jnp.sum(jnp.where(named, route_weights[:, :, None], 0).astype(F32), axis=1)
    table = table.astype(BF16).T
    member = me // 2
    tables = table[None]
    for bit in range(members.bit_length() - 1):
        perm = [(i, i ^ (2 << bit)) for i in range(owners)]
        other = go(tables, perm)
        low = (member >> bit) % 2 == 0
        tables = jnp.where(low, jnp.concatenate([tables, other]), jnp.concatenate([other, tables]))
    order = ring_order(members)
    places = jnp.array([order.index(m) for m in range(members)], jnp.int32)
    offsets = [0]
    for step in range(1, full + 1):
        offsets += [-step, step]
    offsets.append(members // 2)
    place = places[member]
    sources = jnp.array(order, jnp.int32)[(place + jnp.array(offsets, jnp.int32)) % members]
    picked = jnp.take(tables, sources, axis=0).astype(F32)
    pick = jnp.arange(owners, dtype=jnp.int32)[None, :, None]
    weight_own = jnp.sum(jnp.where(pick == me, picked, 0), axis=1).reshape(-1, 1)
    weight_pair = jnp.sum(jnp.where(pick == (me ^ 1), picked, 0), axis=1).reshape(-1, 1)

    pair_scale = go(ia3_scale, pair)
    scales = []
    for low, high in pieces:
        both = [
            lax.dynamic_slice(pair_scale, (0, at + low), (1, high - low))
            for at in (first, half_units - first)
        ]
        scales.append(jnp.concatenate(both, axis=1))
    scale_pair = jnp.concatenate(scales, axis=1)

    token_blocks = gather(tokens)
    cotangent_blocks = gather(cotangent)
    early = 1 + 4 * EARLY
    count = rows * (1 + 2 * EARLY)
    total_rows = rows * members
    spans = (slice(0, count), slice(count, total_rows))
    everything = slice(0, units)

    def shape(height, size, dtype=F32):
        return jax.ShapeDtypeStruct((height, size), dtype)

    owns = []
    for n, group in enumerate((token_blocks[:early], token_blocks[early:])):
        height = spans[n].stop - spans[n].start
        (hidden,) = contract(
            group,
            [[([(w, width)], everything, 0)] for w in (w_gate, w_up)],
            False, [ia3_scale], [shape(height, units, BF16)], finish_own,
        )
        owns.append(hidden)

    pairs = []
    for piece, (low, high) in enumerate(pieces):
        size = 2 * (high - low)
        (hidden,) = contract(
            token_blocks,
            [[([(w, width)], slice(0, size), side * size) for side, w in enumerate(projections[piece])]],
            False, [scales[piece]], [shape(total_rows, size, BF16)], finish_pair,
        )
        pairs.append(hidden)
    takes = [slice(low, high) for low, high in pieces]

    mixed = []
    for chunk, (low, high) in enumerate(bounds):
        total, behind, ahead = both_out(
            owns, pairs, takes, w_down, *downs[chunk], (weight_own, weight_pair), low, split
        )
        ahead = go(ahead, forward)
        behind = go(behind, backward)
        for step in range(full, 0, -1):
            toward, back = hop_sum(total, step, rows, ahead, behind)
            ahead = go(toward, forward)
            behind = go(back, backward)
        mixed.append((total, ahead, behind))
    mixed = last_sum(mixed, rows, bounds)

    grad_own, grad_pair = 0.0, 0.0
    for n, group in enumerate((cotangent_blocks[:early], cotangent_blocks[early:])):
        (grad,) = contract(
            group, [[([(w_down, width)], everything, 0)]], True,
            [weight_own[spans[n]], ia3_scale, owns[n]], [shape(1, units)],
            functools.partial(finish_grad, slice(None)),
        )
        grad_own += grad
        parts, place = [], 0
        for low, high in pieces:
            for side in range(2):
                segments = [(down[side], down[side].shape[1]) for down in downs]
                parts.append((segments, slice(low, high), place))
                place += high - low
        (grad,) = contract(
            group, [parts], True, [weight_pair[spans[n]], scale_pair, *pairs], [shape(1, units)],
            functools.partial(finish_grad, spans[n]),
        )
        grad_pair += grad
    sides, at = ([], []), 0
    for low, high in pieces:
        for side in range(2):
            sides[side].append(grad_pair[:, at : at + high - low])
            at += high - low
    mine, other = (jnp.concatenate(side, axis=1) for side in sides)
    halves = [jnp.concatenate(both, axis=1) for both in ((mine, other), (other, mine))]
    grad_pair = jnp.where(rep == 0, *halves)
    total = grad_own + go(grad_pair, pair)
    total = total + swap(total)
    return mixed, total


def exchanged(tokens, expert_ids, route_weights, cotangent, w_gate, w_up, w_down, ia3_scale):
    owners = lax.axis_size("exp")
    tok_rows, model_width = tokens.shape
    per_token = expert_ids.shape[1]
    capacity = tok_rows * per_token // owners + tok_rows * per_token // (8 * owners)
    flat_ids = expert_ids.reshape(-1)
    one_hot = (flat_ids[:, None] == jnp.arange(owners, dtype=jnp.int32)[None, :]).astype(jnp.int32)
    before = jnp.cumsum(one_hot, axis=0) - one_hot
    slot_index = jnp.sum(before * one_hot, axis=1)
    source_row = jnp.arange(tok_rows * per_token, dtype=jnp.int32) // per_token

    def into_slots(values):
        empty = jnp.zeros((owners, capacity) + values.shape[1:], values.dtype)
        return empty.at[flat_ids, slot_index].set(values)

    token_send = into_slots(tokens[source_row])
    weight_send = into_slots(route_weights.reshape(-1))
    token_recv, weight_recv = (
        lax.all_to_all(token_send, "exp", split_axis=0, concat_axis=0, tiled=True),
        lax.all_to_all(weight_send, "exp", split_axis=0, concat_axis=0, tiled=True),
    )
    received_rows = token_recv.reshape(-1, model_width)
    gate_pre = jnp.dot(received_rows, w_gate[0], preferred_element_type=jnp.float32)
    up_pre = jnp.dot(received_rows, w_up[0], preferred_element_type=jnp.float32)
    activated = jax.nn.silu(gate_pre) * up_pre
    hidden = (ia3_scale[0][None, :] * activated).astype(jnp.bfloat16)
    expert_out = jnp.dot(hidden, w_down[0], preferred_element_type=jnp.float32).astype(jnp.bfloat16)
    returned = lax.all_to_all(
        expert_out.reshape(owners, capacity, model_width),
        "exp",
        split_axis=0,
        concat_axis=0,
        tiled=True,
    )
    picked = returned[flat_ids, slot_index].reshape(tok_rows, per_token, model_width)
    mixed = jnp.einsum(
        "tkd,tk->td", picked, route_weights, preferred_element_type=jnp.float32
    ).astype(jnp.bfloat16)
    grad_send = into_slots(cotangent[source_row])
    grad_recv = lax.all_to_all(grad_send, "exp", split_axis=0, concat_axis=0, tiled=True)
    back_proj = lax.dot_general(
        grad_recv.reshape(-1, model_width),
        w_down[0],
        (((1,), (1,)), ((), ())),
        preferred_element_type=jnp.float32,
    )
    weight_rows = weight_recv.reshape(-1).astype(jnp.float32)
    local_grad = jnp.sum(weight_rows[:, None] * activated * back_proj, axis=0)
    summed = lax.psum(local_grad, "rep")
    return (mixed, summed[None, :])


def dense(owners, per_token):
    return owners in (16,) and 2 * per_token >= owners


def shards(*arrays):
    if not dense(lax.axis_size("exp"), arrays[1].shape[1]):
        return exchanged(*arrays)
    return gathered(*arrays)


def solution(mesh):
    in_specs = (
        P(("rep", "exp"), None),
        P(("rep", "exp"), None),
        P(("rep", "exp"), None),
        P(("rep", "exp"), None),
        P("exp", None, None),
        P("exp", None, None),
        P("exp", None, None),
        P("exp", None),
    )
    out_specs = (P(("rep", "exp"), None), P("exp", None))
    return jax.shard_map(shards, mesh=mesh, in_specs=in_specs, out_specs=out_specs, check_vma=False)
```

```python
import functools
import math

import jax
import jax.numpy as jnp
from jax import lax
from jax.experimental import pallas as pl
from jax.experimental.pallas import tpu as pltpu
from jax.sharding import PartitionSpec as P

TILES = (1, 1, 1)
PIECES = (2, 1)
SHARES = (3, 3, 2)
SLOTS = 3
LANES = 128
EARLY = 2
EARLY_BACK = 1
F32 = jnp.float32
BF16 = jnp.bfloat16
VMEM_LIMIT = 60 * 1024 * 1024
SMALL_LIMIT = 8 * 1024 * 1024


def ring_order(members):
    return list(range(0, members, 2)) + list(reversed(range(1, members, 2)))


def ring_perm(members, step):
    order = ring_order(members)
    perm = []
    for parity in range(2):
        for place, member in enumerate(order):
            target = order[(place + step) % members]
            perm.append((2 * member + parity, 2 * target + parity))
    return perm


def bounds_of(width, shares):
    edges = [0]
    for share in shares:
        edges.append(edges[-1] + width * share // sum(shares))
    return list(zip(edges[:-1], edges[1:]))


def whole(shape):
    return pl.BlockSpec(shape, lambda *_: (0,) * len(shape))


def params():
    return pltpu.CompilerParams(vmem_limit_bytes=VMEM_LIMIT)


def cost(flops, *arrays):
    moved = sum(math.prod(a.shape) * a.dtype.itemsize for a in arrays)
    return pl.CostEstimate(flops=flops, transcendentals=0, bytes_accessed=moved)


def cut_columns(core, w_gate, w_up, low, high):
    depth, units = w_gate.shape
    per_half, tiles = units // 2 // LANES, (high - low) // LANES
    step = math.gcd(depth, 1024)

    def body(core_ref, *refs):
        out_ref = refs[-1]
        for n, ref in enumerate(refs[:-1]):
            out_ref[:, n * LANES : (n + 1) * LANES] = ref[...]

    specs = [
        pl.BlockSpec((step, LANES), lambda i, core_ref, n=n: (i, core_ref[0] * per_half + low // LANES + n))
        for n in range(tiles)
    ]
    out = jax.ShapeDtypeStruct((depth, 2 * (high - low)), w_gate.dtype)
    return pl.pallas_call(
        body,
        out_shape=out,
        grid_spec=pltpu.PrefetchScalarGridSpec(
            num_scalar_prefetch=1,
            grid=(depth // step,),
            in_specs=specs + specs,
            out_specs=pl.BlockSpec((step, 2 * (high - low)), lambda i, core_ref: (i, 0)),
        ),
        cost_estimate=cost(0, out, out),
        compiler_params=params(),
        name="cut_columns",
    )(core, *[w_gate] * tiles, *[w_up] * tiles)


def cut_rows(core, w_down, bounds):
    half, width = w_down.shape[0] // 2, w_down.shape[1]
    step = half // 3 if half % 48 == 0 else half

    def body(core_ref, in_ref, *out_refs):
        for (low, high), out_ref in zip(bounds, out_refs):
            out_ref[...] = in_ref[:, low:high]

    outs = [jax.ShapeDtypeStruct((half, high - low), w_down.dtype) for low, high in bounds]
    return pl.pallas_call(
        body,
        out_shape=outs,
        grid_spec=pltpu.PrefetchScalarGridSpec(
            num_scalar_prefetch=1,
            grid=(half // step,),
            in_specs=[pl.BlockSpec((step, width), lambda i, core_ref: (core_ref[0] * (half // step) + i, 0))],
            out_specs=[pl.BlockSpec((step, high - low), lambda i, core_ref: (i, 0)) for low, high in bounds],
        ),
        cost_estimate=cost(0, *outs, *outs),
        compiler_params=params(),
        name="cut_rows",
    )(core, w_down)


def contract(blocks, groups, transposed, extras, outs, finish):
    starts = [0]
    for block in blocks:
        starts.append(starts[-1] + block.shape[0])
    rows, width = starts[-1], blocks[0].shape[1]
    step = math.gcd(512, width)
    arrays, copies_of, sizes = [], [], []
    for parts in groups:
        size = 0
        for segments, take, place in parts:
            at = 0
            for array, length in segments:
                if not any(array is other for other in arrays):
                    arrays.append(array)
                index = next(i for i, other in enumerate(arrays) if other is array)
                assert length % step == 0
                copies_of.append((len(sizes), index, at // step, length // step, take, place))
                at += length
            size = max(size, place + take.stop - take.start)
        sizes.append(size)
    steps = width // step
    count, parts_count = len(blocks), len(copies_of)
    slots = min(SLOTS, steps)

    def body(*refs):
        block_refs, refs = refs[:count], refs[count:]
        array_refs, refs = refs[: len(arrays)], refs[len(arrays) :]
        extra_refs, refs = refs[: len(extras)], refs[len(extras) :]
        out_refs, refs = refs[: len(outs)], refs[len(outs) :]
        held, sems, weight_sems, refs = refs[0], refs[1], refs[2], refs[3:]
        weight_refs, totals = refs[: len(sizes)], refs[len(sizes) :]
        k = pl.program_id(0)

        def block_copies(at, slot):
            columns = pl.ds(pl.multiple_of(at * step, step), step)
            return [
                pltpu.make_async_copy(
                    ref.at[:, columns],
                    held.at[slot, pl.ds(starts[i], blocks[i].shape[0]), :],
                    sems.at[slot, i],
                )
                for i, ref in enumerate(block_refs)
            ]

        def weight_copy(part, at, slot):
            j, index, first, _, take, place = copies_of[part]
            along = pl.ds(pl.multiple_of((at - first) * step, step), step)
            across = pl.ds(take.start, take.stop - take.start)
            there = pl.ds(place, take.stop - take.start)
            if transposed:
                source, target = array_refs[index].at[across, along], weight_refs[j].at[slot, there, :]
            else:
                source, target = array_refs[index].at[along, across], weight_refs[j].at[slot, :, there]
            return pltpu.make_async_copy(source, target, weight_sems.at[slot, part])

        def each(at, slot, do):
            for copy in block_copies(at, slot):
                do(copy)
            for part, (_, _, first, length, _, _) in enumerate(copies_of):
                if length == steps:
                    do(weight_copy(part, at, slot))
                else:

                    @pl.when((at >= first) & (at < first + length))
                    def _():
                        do(weight_copy(part, at, slot))

        slot = lax.rem(k, slots)

        @pl.when(k == 0)
        def _():
            for early in range(slots - 1):
                each(early, early, lambda copy: copy.start())

        @pl.when(k + slots - 1 < steps)
        def _():
            each(k + slots - 1, lax.rem(k + slots - 1, slots), lambda copy: copy.start())

        each(k, slot, lambda copy: copy.wait())
        dims = (((1,), (1 if transposed else 0,)), ((), ()))

        def product(j):
            return lax.dot_general(held[slot], weight_refs[j][slot], dims, preferred_element_type=F32)

        @pl.when(k == 0)
        def _():
            for j, total in enumerate(totals):
                total[...] = product(j)

        @pl.when(k > 0)
        def _():
            for j, total in enumerate(totals):
                total[...] += product(j)

        @pl.when(k == steps - 1)
        def _():
            finish(totals, extra_refs, out_refs)

    specs = [pl.BlockSpec(memory_space=pltpu.HBM)] * (count + len(arrays))
    specs += [pl.BlockSpec(a.shape, lambda k: (0, 0), pipeline_mode=pl.Buffered(1)) for a in extras]
    dtype = blocks[0].dtype
    return pl.pallas_call(
        body,
        out_shape=outs,
        grid=(steps,),
        in_specs=specs,
        out_specs=[whole(out.shape) for out in outs],
        scratch_shapes=[
            pltpu.VMEM((slots, rows, step), dtype),
            pltpu.SemaphoreType.DMA((slots, count)),
            pltpu.SemaphoreType.DMA((slots, parts_count)),
            *[pltpu.VMEM((slots, size, step) if transposed else (slots, step, size), dtype) for size in sizes],
            *[pltpu.VMEM((rows, size), F32) for size in sizes],
        ],
        compiler_params=params(),
        cost_estimate=cost(2 * rows * sum(sizes) * width, *outs),
    )(*blocks, *arrays, *extras)


def silu(v):
    return v / (1.0 + jnp.exp(-v))


def finish_own(totals, extra_refs, out_refs):
    act = silu(totals[0][...]) * totals[1][...]
    out_refs[0][...] = (extra_refs[0][...] * act).astype(BF16)


def finish_pair(totals, extra_refs, out_refs):
    total = totals[0]
    size = total.shape[1] // 4
    for side in range(2):
        gate, up = total[:, 2 * side * size : (2 * side + 1) * size], total[:, (2 * side + 1) * size : (2 * side + 2) * size]
        columns = slice(side * size, (side + 1) * size)
        out_refs[0][:, columns] = (extra_refs[0][:, columns] * (silu(gate) * up)).astype(BF16)


def finish_grad(span, totals, extra_refs, out_refs):
    weight, scale, hiddens = extra_refs[0], extra_refs[1], extra_refs[2:]
    first = 0
    for hidden in hiddens:
        columns = slice(first, first + hidden.shape[1])
        term = weight[...] * hidden[span, :].astype(F32) * totals[0][:, columns]
        out_refs[0][:, columns] = jnp.sum(term, axis=0, keepdims=True) / scale[:, columns]
        first += hidden.shape[1]


def both_out(owns, pairs, takes, w_down, mine, other, weights, low, split):
    rows = sum(own.shape[0] for own in owns)
    heights = [2 * split] * (rows // split // 2 - 1) + [split, split]
    units = w_down.shape[0]
    width = mine.shape[1]
    step = math.gcd(math.gcd(low, width), 512)

    def body(*refs):
        own_refs, refs = refs[: len(owns)], refs[len(owns) :]
        pair_refs, refs = refs[: len(pairs)], refs[len(pairs) :]
        w_ref, mine_ref, other_ref, weight_own, weight_pair, *out_refs, hidden = refs

        @pl.when(pl.program_id(0) == 0)
        def _():
            done = 0
            for ref in own_refs:
                hidden[0, done : done + ref.shape[0], :] = ref[...]
                done += ref.shape[0]
            done = 0
            for ref in pair_refs:
                hidden[1, :, done : done + ref.shape[1]] = ref[...]
                done += ref.shape[1]

        w = jnp.concatenate([ref[take, :] for take in takes for ref in (mine_ref, other_ref)], axis=0)
        total = weight_own[...] * jnp.dot(hidden[0], w_ref[...], preferred_element_type=F32)
        total += weight_pair[...] * jnp.dot(hidden[1], w, preferred_element_type=F32)
        total = total.astype(BF16)
        done = 0
        for out_ref in out_refs:
            out_ref[...] = total[done : done + out_ref.shape[0]]
            done += out_ref.shape[0]

    def columns(height, first=0):
        return pl.BlockSpec((height, step), lambda j: (0, first // step + j))

    def fixed(a):
        return pl.BlockSpec(a.shape, lambda j: (0, 0), pipeline_mode=pl.Buffered(1))

    outs = [jax.ShapeDtypeStruct((height, width), BF16) for height in heights]
    return pl.pallas_call(
        body,
        out_shape=outs,
        grid=(width // step,),
        in_specs=[fixed(a) for a in (*owns, *pairs)]
        + [columns(units, low), columns(mine.shape[0]), columns(mine.shape[0])]
        + [fixed(a) for a in weights],
        out_specs=[columns(height) for height in heights],
        scratch_shapes=[pltpu.VMEM((2, rows, units), BF16)],
        compiler_params=params(),
        cost_estimate=cost(4 * rows * units * width, *outs),
    )(*owns, *pairs, w_down, mine, other, *weights)


def hop_sum(near, far, ahead, behind):
    rows, width = near.shape
    split = ahead.shape[0]

    def body(near_ref, far_ref, ahead_ref, behind_ref, out_toward, out_back, toward, back, fore, aft, sems):
        sources = (near_ref, far_ref, ahead_ref, behind_ref)
        copies = [
            pltpu.make_async_copy(source, target, sems.at[i])
            for i, (source, target) in enumerate(zip(sources, (toward, back, fore, aft)))
        ]
        for copy in copies:
            copy.start()
        for copy in copies:
            copy.wait()
        low, high = (slice(None), slice(None)) if split == rows else (slice(0, split), slice(split, rows))
        if split != rows:
            out_toward[low, :] = toward[low, :]
            out_back[high, :] = back[high, :]
        out_toward[high, :] = (toward[high, :].astype(F32) + fore[...].astype(F32)).astype(BF16)
        out_back[low, :] = (back[low, :].astype(F32) + aft[...].astype(F32)).astype(BF16)

    out = jax.ShapeDtypeStruct((rows, width), BF16)
    return pl.pallas_call(
        body,
        out_shape=[out, out],
        grid=(1,),
        in_specs=[pl.BlockSpec(memory_space=pltpu.HBM)] * 4,
        out_specs=[whole(out.shape)] * 2,
        scratch_shapes=[
            pltpu.VMEM(out.shape, BF16),
            pltpu.VMEM(out.shape, BF16),
            pltpu.VMEM(ahead.shape, BF16),
            pltpu.VMEM(behind.shape, BF16),
            pltpu.SemaphoreType.DMA((4,)),
        ],
        compiler_params=pltpu.CompilerParams(vmem_limit_bytes=SMALL_LIMIT),
        cost_estimate=cost(0, out, out, out, out),
    )(near, far, ahead, behind)


def last_sum(chunks, rows, bounds):
    flat = [a for chunk in chunks for a in chunk]

    def body(*refs):
        out_ref, held, sems = refs[len(flat) :]
        copies = []
        for n, (low, high) in enumerate(bounds):
            for i, ref in enumerate(refs[3 * n : 3 * n + 3]):
                source = ref.at[pl.ds(0, rows), :]
                copies.append(pltpu.make_async_copy(source, held.at[i, :, pl.ds(low, high - low)], sems.at[n, i]))
        for copy in copies:
            copy.start()
        for copy in copies:
            copy.wait()
        total = held[0].astype(F32) + held[1].astype(F32) + held[2].astype(F32)
        out_ref[...] = total.astype(BF16)

    out = jax.ShapeDtypeStruct((rows, bounds[-1][1]), BF16)
    return pl.pallas_call(
        body,
        out_shape=out,
        grid=(1,),
        in_specs=[pl.BlockSpec(memory_space=pltpu.HBM)] * len(flat),
        out_specs=whole(out.shape),
        scratch_shapes=[
            pltpu.VMEM((3, *out.shape), BF16),
            pltpu.SemaphoreType.DMA((len(bounds), 3)),
        ],
        compiler_params=pltpu.CompilerParams(vmem_limit_bytes=SMALL_LIMIT),
        cost_estimate=cost(0, out, out, out, out),
    )(*flat)


def gathered(tokens, expert_ids, route_weights, cotangent, w_gate, w_up, w_down, ia3_scale):
    owners = lax.axis_size("exp")
    members = owners // 2
    rows, width = tokens.shape
    units = w_gate.shape[2]
    half_units = units // 2
    me = lax.axis_index("exp")
    rep = lax.axis_index("rep")
    w_gate, w_up, w_down = w_gate[0], w_up[0], w_down[0]
    forward, backward = ring_perm(members, 1), ring_perm(members, -1)
    pair = [(i, i ^ 1) for i in range(owners)]
    cores = [(0, 1), (1, 0)]
    full = members // 2 - 1
    split = rows // 2

    def go(value, perm):
        return lax.ppermute(value, "exp", perm)

    def swap(value):
        return lax.ppermute(value, "rep", cores)

    def gather(block):
        halves = (block[:split], block[split:])
        ahead, behind = list(halves), list(halves)
        blocks = [block]
        for _ in range(1, full + 1):
            ahead = [go(ahead[h], forward) for h in range(2)]
            behind = [go(behind[h], backward) for h in range(2)]
            blocks += ahead + behind
        blocks.append(go(ahead[0], forward))
        blocks.append(go(behind[1], backward))
        return blocks

    pieces = bounds_of(half_units, PIECES)
    first = rep * half_units
    core = jnp.full((1,), rep, jnp.int32)
    projections = []
    for low, high in bounds_of(half_units, TILES):
        cut = cut_columns(core, w_gate, w_up, low, high)
        mine = go(cut, pair)
        projections.append((low, high, mine, swap(mine)))
    bounds = bounds_of(width, SHARES)
    cuts = cut_rows(core, w_down, bounds)
    downs = []
    for cut in cuts:
        mine = go(cut, pair)
        downs.append((mine, swap(mine)))

    named = expert_ids[:, :, None] == jnp.arange(owners, dtype=jnp.int32)
    table = jnp.sum(jnp.where(named, route_weights[:, :, None], 0).astype(F32), axis=1)
    table = table.astype(BF16).T
    member = me // 2
    tables = table[None]
    for bit in range(members.bit_length() - 1):
        perm = [(i, i ^ (2 << bit)) for i in range(owners)]
        other = go(tables, perm)
        low = (member >> bit) % 2 == 0
        tables = jnp.where(low, jnp.concatenate([tables, other]), jnp.concatenate([other, tables]))
    order = ring_order(members)
    places = jnp.array([order.index(m) for m in range(members)], jnp.int32)
    offsets = [0]
    for step in range(1, full + 1):
        offsets += [-step, step]
    offsets.append(members // 2)
    place = places[member]
    sources = jnp.array(order, jnp.int32)[(place + jnp.array(offsets, jnp.int32)) % members]
    picked = jnp.take(tables, sources, axis=0).astype(F32)
    pick = jnp.arange(owners, dtype=jnp.int32)[None, :, None]
    weight_own = jnp.sum(jnp.where(pick == me, picked, 0), axis=1).reshape(-1, 1)
    weight_pair = jnp.sum(jnp.where(pick == (me ^ 1), picked, 0), axis=1).reshape(-1, 1)

    pair_scale = go(ia3_scale, pair)
    scales = []
    for low, high in pieces:
        both = [
            lax.dynamic_slice(pair_scale, (0, at + low), (1, high - low))
            for at in (first, half_units - first)
        ]
        scales.append(jnp.concatenate(both, axis=1))
    scale_pair = jnp.concatenate(scales, axis=1)

    token_blocks = gather(tokens)
    cotangent_blocks = gather(cotangent)
    early = 1 + 4 * EARLY
    count = rows * (1 + 2 * EARLY)
    total_rows = rows * members
    spans = (slice(0, count), slice(count, total_rows))
    everything = slice(0, units)

    def shape(height, size, dtype=F32):
        return jax.ShapeDtypeStruct((height, size), dtype)

    owns = []
    for n, group in enumerate((token_blocks[:early], token_blocks[early:])):
        height = spans[n].stop - spans[n].start
        (hidden,) = contract(
            group,
            [[([(w, width)], everything, 0)] for w in (w_gate, w_up)],
            False, [ia3_scale], [shape(height, units, BF16)], finish_own,
        )
        owns.append(hidden)

    pairs = []
    for piece, (low, high) in enumerate(pieces):
        size = high - low
        parts = []
        for start, stop, *arrays in projections:
            if low <= start < high:
                for side, array in enumerate(arrays):
                    for half in range(2):
                        take = slice(half * (stop - start), (half + 1) * (stop - start))
                        parts.append(([(array, width)], take, (2 * side + half) * size + start - low))
        (hidden,) = contract(
            token_blocks, [parts], False, [scales[piece]], [shape(total_rows, 2 * size, BF16)],
            finish_pair,
        )
        pairs.append(hidden)
    takes = [slice(low, high) for low, high in pieces]

    mixed = []
    for chunk, (low, high) in enumerate(bounds):
        *blocks, behind, ahead = both_out(
            owns, pairs, takes, w_down, *downs[chunk], (weight_own, weight_pair), low, split
        )
        ahead = go(ahead, forward)
        behind = go(behind, backward)
        for step in range(full, 0, -1):
            toward, back = hop_sum(blocks[2 * step], blocks[2 * step - 1], ahead, behind)
            ahead = go(toward, forward)
            behind = go(back, backward)
        mixed.append((blocks[0], ahead, behind))
    mixed = last_sum(mixed, rows, bounds)

    grad_own = 0.0
    early_back = 1 + 4 * EARLY_BACK
    middle = rows * (1 + 2 * EARLY_BACK)
    for n, (group, span) in enumerate(
        (
            (cotangent_blocks[:early_back], slice(0, middle)),
            (cotangent_blocks[early_back:], slice(middle, total_rows)),
        )
    ):
        hidden_rows = owns[0] if n == 0 else jnp.concatenate([owns[0][middle:], owns[1]])
        (grad,) = contract(
            group, [[([(w_down, width)], everything, 0)]], True,
            [weight_own[span], ia3_scale, hidden_rows], [shape(1, units)],
            functools.partial(finish_grad, slice(0, span.stop - span.start)),
        )
        grad_own += grad
    parts, place = [], 0
    for low, high in pieces:
        for side in range(2):
            segments = [(down[side], down[side].shape[1]) for down in downs]
            parts.append((segments, slice(low, high), place))
            place += high - low
    (grad_pair,) = contract(
        cotangent_blocks, [parts], True, [weight_pair, scale_pair, *pairs], [shape(1, units)],
        functools.partial(finish_grad, slice(None)),
    )
    sides, at = ([], []), 0
    for low, high in pieces:
        for side in range(2):
            sides[side].append(grad_pair[:, at : at + high - low])
            at += high - low
    mine, other = (jnp.concatenate(side, axis=1) for side in sides)
    halves = [jnp.concatenate(both, axis=1) for both in ((mine, other), (other, mine))]
    grad_pair = jnp.where(rep == 0, *halves)
    total = grad_own + go(grad_pair, pair)
    total = total + swap(total)
    return mixed, total


def exchanged(tokens, expert_ids, route_weights, cotangent, w_gate, w_up, w_down, ia3_scale):
    owners = lax.axis_size("exp")
    tok_rows, model_width = tokens.shape
    per_token = expert_ids.shape[1]
    capacity = tok_rows * per_token // owners + tok_rows * per_token // (8 * owners)
    flat_ids = expert_ids.reshape(-1)
    one_hot = (flat_ids[:, None] == jnp.arange(owners, dtype=jnp.int32)[None, :]).astype(jnp.int32)
    before = jnp.cumsum(one_hot, axis=0) - one_hot
    slot_index = jnp.sum(before * one_hot, axis=1)
    source_row = jnp.arange(tok_rows * per_token, dtype=jnp.int32) // per_token

    def into_slots(values):
        empty = jnp.zeros((owners, capacity) + values.shape[1:], values.dtype)
        return empty.at[flat_ids, slot_index].set(values)

    token_send = into_slots(tokens[source_row])
    weight_send = into_slots(route_weights.reshape(-1))
    token_recv, weight_recv = (
        lax.all_to_all(token_send, "exp", split_axis=0, concat_axis=0, tiled=True),
        lax.all_to_all(weight_send, "exp", split_axis=0, concat_axis=0, tiled=True),
    )
    received_rows = token_recv.reshape(-1, model_width)
    gate_pre = jnp.dot(received_rows, w_gate[0], preferred_element_type=jnp.float32)
    up_pre = jnp.dot(received_rows, w_up[0], preferred_element_type=jnp.float32)
    activated = jax.nn.silu(gate_pre) * up_pre
    hidden = (ia3_scale[0][None, :] * activated).astype(jnp.bfloat16)
    expert_out = jnp.dot(hidden, w_down[0], preferred_element_type=jnp.float32).astype(jnp.bfloat16)
    returned = lax.all_to_all(
        expert_out.reshape(owners, capacity, model_width),
        "exp",
        split_axis=0,
        concat_axis=0,
        tiled=True,
    )
    picked = returned[flat_ids, slot_index].reshape(tok_rows, per_token, model_width)
    mixed = jnp.einsum(
        "tkd,tk->td", picked, route_weights, preferred_element_type=jnp.float32
    ).astype(jnp.bfloat16)
    grad_send = into_slots(cotangent[source_row])
    grad_recv = lax.all_to_all(grad_send, "exp", split_axis=0, concat_axis=0, tiled=True)
    back_proj = lax.dot_general(
        grad_recv.reshape(-1, model_width),
        w_down[0],
        (((1,), (1,)), ((), ())),
        preferred_element_type=jnp.float32,
    )
    weight_rows = weight_recv.reshape(-1).astype(jnp.float32)
    local_grad = jnp.sum(weight_rows[:, None] * activated * back_proj, axis=0)
    summed = lax.psum(local_grad, "rep")
    return (mixed, summed[None, :])


def dense(owners, per_token):
    return owners in (16,) and 2 * per_token >= owners


def shards(*arrays):
    if not dense(lax.axis_size("exp"), arrays[1].shape[1]):
        return exchanged(*arrays)
    return gathered(*arrays)


def solution(mesh):
    in_specs = (
        P(("rep", "exp"), None),
        P(("rep", "exp"), None),
        P(("rep", "exp"), None),
        P(("rep", "exp"), None),
        P("exp", None, None),
        P("exp", None, None),
        P("exp", None, None),
        P("exp", None),
    )
    out_specs = (P(("rep", "exp"), None), P("exp", None))
    return jax.shard_map(shards, mesh=mesh, in_specs=in_specs, out_specs=out_specs, check_vma=False)
```

```python
import functools
import math

import jax
import jax.numpy as jnp
from jax import lax
from jax.experimental import pallas as pl
from jax.experimental.pallas import tpu as pltpu
from jax.sharding import PartitionSpec as P

TILES = (1, 1, 1)
PIECES = (2, 1)
SHARES = (3, 3, 2)
SLOTS = 3
LANES = 128
EARLY = 2
EARLY_BACK = 1
F32 = jnp.float32
BF16 = jnp.bfloat16
VMEM_LIMIT = 60 * 1024 * 1024
SMALL_LIMIT = 8 * 1024 * 1024


def ring_order(members):
    return list(range(0, members, 2)) + list(reversed(range(1, members, 2)))


def ring_perm(members, step):
    order = ring_order(members)
    perm = []
    for parity in range(2):
        for place, member in enumerate(order):
            target = order[(place + step) % members]
            perm.append((2 * member + parity, 2 * target + parity))
    return perm


def bounds_of(width, shares):
    edges = [0]
    for share in shares:
        edges.append(edges[-1] + width * share // sum(shares))
    return list(zip(edges[:-1], edges[1:]))


def whole(shape):
    return pl.BlockSpec(shape, lambda *_: (0,) * len(shape))


def params():
    return pltpu.CompilerParams(vmem_limit_bytes=VMEM_LIMIT)


def cost(flops, *arrays):
    moved = sum(math.prod(a.shape) * a.dtype.itemsize for a in arrays)
    return pl.CostEstimate(flops=flops, transcendentals=0, bytes_accessed=moved)


def cut_columns(core, w_gate, w_up, low, high):
    depth, units = w_gate.shape
    half, size = units // 2, high - low
    step = math.gcd(depth, 1024)
    steps = depth // step

    def body(core_ref, gate_ref, up_ref, out_ref, held, sems, out_sems):
        first = pl.multiple_of(core_ref[0] * half + low, LANES)
        ins, outs = [], []
        for i in range(steps):
            span = pl.ds(i * step, step)
            for n, ref in enumerate((gate_ref, up_ref)):
                source = ref.at[span, pl.ds(first, size)]
                ins.append(pltpu.make_async_copy(source, held.at[span, pl.ds(n * size, size)], sems.at[i, n]))
            outs.append(pltpu.make_async_copy(held.at[span, :], out_ref.at[span, :], out_sems.at[i]))
        for copy in ins:
            copy.start()
        for i in range(steps):
            ins[2 * i].wait()
            ins[2 * i + 1].wait()
            outs[i].start()
        for copy in outs:
            copy.wait()

    out = jax.ShapeDtypeStruct((depth, 2 * size), w_gate.dtype)
    return pl.pallas_call(
        body,
        out_shape=out,
        grid_spec=pltpu.PrefetchScalarGridSpec(
            num_scalar_prefetch=1,
            grid=(1,),
            in_specs=[pl.BlockSpec(memory_space=pltpu.HBM)] * 2,
            out_specs=pl.BlockSpec(memory_space=pltpu.HBM),
            scratch_shapes=[
                pltpu.VMEM(out.shape, out.dtype),
                pltpu.SemaphoreType.DMA((steps, 2)),
                pltpu.SemaphoreType.DMA((steps,)),
            ],
        ),
        compiler_params=params(),
        cost_estimate=cost(0, out, out),
        name="cut_columns",
    )(core, w_gate, w_up)


def cut_rows(core, w_down, bounds):
    half, width = w_down.shape[0] // 2, w_down.shape[1]
    step = half // 3 if half % 48 == 0 else half

    def body(core_ref, in_ref, *out_refs):
        for (low, high), out_ref in zip(bounds, out_refs):
            out_ref[...] = in_ref[:, low:high]

    outs = [jax.ShapeDtypeStruct((half, high - low), w_down.dtype) for low, high in bounds]
    return pl.pallas_call(
        body,
        out_shape=outs,
        grid_spec=pltpu.PrefetchScalarGridSpec(
            num_scalar_prefetch=1,
            grid=(half // step,),
            in_specs=[pl.BlockSpec((step, width), lambda i, core_ref: (core_ref[0] * (half // step) + i, 0))],
            out_specs=[pl.BlockSpec((step, high - low), lambda i, core_ref: (i, 0)) for low, high in bounds],
        ),
        cost_estimate=cost(0, *outs, *outs),
        compiler_params=params(),
        name="cut_rows",
    )(core, w_down)


def contract(blocks, groups, transposed, extras, outs, finish):
    starts = [0]
    for block in blocks:
        starts.append(starts[-1] + block.shape[0])
    rows, width = starts[-1], blocks[0].shape[1]
    lengths = [length for parts in groups for segments, _, _ in parts for _, length in segments]
    step = math.gcd(1024, width, *lengths)
    arrays, copies_of, sizes = [], [], []
    for parts in groups:
        size = 0
        for segments, take, place in parts:
            at = 0
            for array, length in segments:
                if not any(array is other for other in arrays):
                    arrays.append(array)
                index = next(i for i, other in enumerate(arrays) if other is array)
                assert length % step == 0
                copies_of.append((len(sizes), index, at // step, length // step, take, place))
                at += length
            size = max(size, place + take.stop - take.start)
        sizes.append(size)
    steps = width // step
    count, parts_count = len(blocks), len(copies_of)
    slots = min(SLOTS, steps)

    def body(*refs):
        block_refs, refs = refs[:count], refs[count:]
        array_refs, refs = refs[: len(arrays)], refs[len(arrays) :]
        extra_refs, refs = refs[: len(extras)], refs[len(extras) :]
        out_refs, refs = refs[: len(outs)], refs[len(outs) :]
        held, sems, weight_sems, refs = refs[0], refs[1], refs[2], refs[3:]
        weight_refs, totals = refs[: len(sizes)], refs[len(sizes) :]
        k = pl.program_id(0)

        def block_copies(at, slot):
            columns = pl.ds(pl.multiple_of(at * step, step), step)
            return [
                pltpu.make_async_copy(
                    ref.at[:, columns],
                    held.at[slot, pl.ds(starts[i], blocks[i].shape[0]), :],
                    sems.at[slot, i],
                )
                for i, ref in enumerate(block_refs)
            ]

        def weight_copy(part, at, slot):
            j, index, first, _, take, place = copies_of[part]
            along = pl.ds(pl.multiple_of((at - first) * step, step), step)
            across = pl.ds(take.start, take.stop - take.start)
            there = pl.ds(place, take.stop - take.start)
            if transposed:
                source, target = array_refs[index].at[across, along], weight_refs[j].at[slot, there, :]
            else:
                source, target = array_refs[index].at[along, across], weight_refs[j].at[slot, :, there]
            return pltpu.make_async_copy(source, target, weight_sems.at[slot, part])

        def each(at, slot, do):
            for copy in block_copies(at, slot):
                do(copy)
            for part, (_, _, first, length, _, _) in enumerate(copies_of):
                if length == steps:
                    do(weight_copy(part, at, slot))
                else:

                    @pl.when((at >= first) & (at < first + length))
                    def _():
                        do(weight_copy(part, at, slot))

        slot = lax.rem(k, slots)

        @pl.when(k == 0)
        def _():
            for early in range(slots - 1):
                each(early, early, lambda copy: copy.start())

        @pl.when(k + slots - 1 < steps)
        def _():
            each(k + slots - 1, lax.rem(k + slots - 1, slots), lambda copy: copy.start())

        each(k, slot, lambda copy: copy.wait())
        dims = (((1,), (1 if transposed else 0,)), ((), ()))

        def product(j):
            return lax.dot_general(held[slot], weight_refs[j][slot], dims, preferred_element_type=F32)

        @pl.when(k == 0)
        def _():
            for j, total in enumerate(totals):
                total[...] = product(j)

        @pl.when(k > 0)
        def _():
            for j, total in enumerate(totals):
                total[...] += product(j)

        @pl.when(k == steps - 1)
        def _():
            finish(totals, extra_refs, out_refs)

    specs = [pl.BlockSpec(memory_space=pltpu.HBM)] * (count + len(arrays))
    specs += [pl.BlockSpec(a.shape, lambda k: (0, 0), pipeline_mode=pl.Buffered(1)) for a in extras]
    dtype = blocks[0].dtype
    return pl.pallas_call(
        body,
        out_shape=outs,
        grid=(steps,),
        in_specs=specs,
        out_specs=[whole(out.shape) for out in outs],
        scratch_shapes=[
            pltpu.VMEM((slots, rows, step), dtype),
            pltpu.SemaphoreType.DMA((slots, count)),
            pltpu.SemaphoreType.DMA((slots, parts_count)),
            *[pltpu.VMEM((slots, size, step) if transposed else (slots, step, size), dtype) for size in sizes],
            *[pltpu.VMEM((rows, size), F32) for size in sizes],
        ],
        compiler_params=params(),
        cost_estimate=cost(2 * rows * sum(sizes) * width, *outs),
    )(*blocks, *arrays, *extras)


def silu(v):
    return v / (1.0 + jnp.exp(-v))


def finish_own(totals, extra_refs, out_refs):
    act = silu(totals[0][...]) * totals[1][...]
    out_refs[0][...] = (extra_refs[0][...] * act).astype(BF16)


def finish_pair(totals, extra_refs, out_refs):
    total = totals[0]
    size = total.shape[1] // 4
    for side in range(2):
        gate, up = total[:, 2 * side * size : (2 * side + 1) * size], total[:, (2 * side + 1) * size : (2 * side + 2) * size]
        columns = slice(side * size, (side + 1) * size)
        out_refs[0][:, columns] = (extra_refs[0][:, columns] * (silu(gate) * up)).astype(BF16)


def finish_grad(span, totals, extra_refs, out_refs):
    weight, scale, hiddens = extra_refs[0], extra_refs[1], extra_refs[2:]
    first = 0
    for hidden in hiddens:
        columns = slice(first, first + hidden.shape[1])
        term = weight[...] * hidden[span, :].astype(F32) * totals[0][:, columns]
        out_refs[0][:, columns] = jnp.sum(term, axis=0, keepdims=True) / scale[:, columns]
        first += hidden.shape[1]


def both_out(owns, pairs, takes, w_down, mine, other, weights, low, split):
    rows = sum(own.shape[0] for own in owns)
    heights = [2 * split] * (rows // split // 2 - 1) + [split, split]
    units = w_down.shape[0]
    width = mine.shape[1]
    step = math.gcd(math.gcd(low, width), 512)

    def body(*refs):
        own_refs, refs = refs[: len(owns)], refs[len(owns) :]
        pair_refs, refs = refs[: len(pairs)], refs[len(pairs) :]
        w_ref, mine_ref, other_ref, weight_own, weight_pair, *out_refs, hidden = refs

        @pl.when(pl.program_id(0) == 0)
        def _():
            done = 0
            for ref in own_refs:
                hidden[0, done : done + ref.shape[0], :] = ref[...]
                done += ref.shape[0]
            done = 0
            for ref in pair_refs:
                hidden[1, :, done : done + ref.shape[1]] = ref[...]
                done += ref.shape[1]

        w = jnp.concatenate([ref[take, :] for take in takes for ref in (mine_ref, other_ref)], axis=0)
        total = weight_own[...] * jnp.dot(hidden[0], w_ref[...], preferred_element_type=F32)
        total += weight_pair[...] * jnp.dot(hidden[1], w, preferred_element_type=F32)
        total = total.astype(BF16)
        done = 0
        for out_ref in out_refs:
            out_ref[...] = total[done : done + out_ref.shape[0]]
            done += out_ref.shape[0]

    def columns(height, first=0):
        return pl.BlockSpec((height, step), lambda j: (0, first // step + j))

    def fixed(a):
        return pl.BlockSpec(a.shape, lambda j: (0, 0), pipeline_mode=pl.Buffered(1))

    outs = [jax.ShapeDtypeStruct((height, width), BF16) for height in heights]
    return pl.pallas_call(
        body,
        out_shape=outs,
        grid=(width // step,),
        in_specs=[fixed(a) for a in (*owns, *pairs)]
        + [columns(units, low), columns(mine.shape[0]), columns(mine.shape[0])]
        + [fixed(a) for a in weights],
        out_specs=[columns(height) for height in heights],
        scratch_shapes=[pltpu.VMEM((2, rows, units), BF16)],
        compiler_params=params(),
        cost_estimate=cost(4 * rows * units * width, *outs),
    )(*owns, *pairs, w_down, mine, other, *weights)


def hop_sum(near, far, ahead, behind):
    rows, width = near.shape
    split = ahead.shape[0]

    def body(near_ref, far_ref, ahead_ref, behind_ref, out_toward, out_back, toward, back, fore, aft, sems):
        sources = (near_ref, far_ref, ahead_ref, behind_ref)
        copies = [
            pltpu.make_async_copy(source, target, sems.at[i])
            for i, (source, target) in enumerate(zip(sources, (toward, back, fore, aft)))
        ]
        for copy in copies:
            copy.start()
        for copy in copies:
            copy.wait()
        low, high = (slice(None), slice(None)) if split == rows else (slice(0, split), slice(split, rows))
        if split != rows:
            out_toward[low, :] = toward[low, :]
            out_back[high, :] = back[high, :]
        out_toward[high, :] = (toward[high, :].astype(F32) + fore[...].astype(F32)).astype(BF16)
        out_back[low, :] = (back[low, :].astype(F32) + aft[...].astype(F32)).astype(BF16)

    out = jax.ShapeDtypeStruct((rows, width), BF16)
    return pl.pallas_call(
        body,
        out_shape=[out, out],
        grid=(1,),
        in_specs=[pl.BlockSpec(memory_space=pltpu.HBM)] * 4,
        out_specs=[whole(out.shape)] * 2,
        scratch_shapes=[
            pltpu.VMEM(out.shape, BF16),
            pltpu.VMEM(out.shape, BF16),
            pltpu.VMEM(ahead.shape, BF16),
            pltpu.VMEM(behind.shape, BF16),
            pltpu.SemaphoreType.DMA((4,)),
        ],
        compiler_params=pltpu.CompilerParams(vmem_limit_bytes=SMALL_LIMIT),
        cost_estimate=cost(0, out, out, out, out),
    )(near, far, ahead, behind)


def last_sum(chunks, rows, bounds):
    flat = [a for chunk in chunks for a in chunk]

    def body(*refs):
        out_ref, held, sems = refs[len(flat) :]
        copies = []
        for n, (low, high) in enumerate(bounds):
            for i, ref in enumerate(refs[3 * n : 3 * n + 3]):
                source = ref.at[pl.ds(0, rows), :]
                copies.append(pltpu.make_async_copy(source, held.at[i, :, pl.ds(low, high - low)], sems.at[n, i]))
        for copy in copies:
            copy.start()
        for copy in copies:
            copy.wait()
        total = held[0].astype(F32) + held[1].astype(F32) + held[2].astype(F32)
        out_ref[...] = total.astype(BF16)

    out = jax.ShapeDtypeStruct((rows, bounds[-1][1]), BF16)
    return pl.pallas_call(
        body,
        out_shape=out,
        grid=(1,),
        in_specs=[pl.BlockSpec(memory_space=pltpu.HBM)] * len(flat),
        out_specs=whole(out.shape),
        scratch_shapes=[
            pltpu.VMEM((3, *out.shape), BF16),
            pltpu.SemaphoreType.DMA((len(bounds), 3)),
        ],
        compiler_params=pltpu.CompilerParams(vmem_limit_bytes=SMALL_LIMIT),
        cost_estimate=cost(0, out, out, out, out),
    )(*flat)


def gathered(tokens, expert_ids, route_weights, cotangent, w_gate, w_up, w_down, ia3_scale):
    owners = lax.axis_size("exp")
    members = owners // 2
    rows, width = tokens.shape
    units = w_gate.shape[2]
    half_units = units // 2
    me = lax.axis_index("exp")
    rep = lax.axis_index("rep")
    w_gate, w_up, w_down = w_gate[0], w_up[0], w_down[0]
    forward, backward = ring_perm(members, 1), ring_perm(members, -1)
    pair = [(i, i ^ 1) for i in range(owners)]
    cores = [(0, 1), (1, 0)]
    full = members // 2 - 1
    split = rows // 2

    def go(value, perm):
        return lax.ppermute(value, "exp", perm)

    def swap(value):
        return lax.ppermute(value, "rep", cores)

    def gather(block):
        halves = (block[:split], block[split:])
        ahead, behind = list(halves), list(halves)
        blocks = [block]
        for _ in range(1, full + 1):
            ahead = [go(ahead[h], forward) for h in range(2)]
            behind = [go(behind[h], backward) for h in range(2)]
            blocks += ahead + behind
        blocks.append(go(ahead[0], forward))
        blocks.append(go(behind[1], backward))
        return blocks

    pieces = bounds_of(half_units, PIECES)
    first = rep * half_units
    core = jnp.full((1,), rep, jnp.int32)
    projections = []
    for low, high in bounds_of(half_units, TILES):
        cut = cut_columns(core, w_gate, w_up, low, high)
        mine = go(cut, pair)
        projections.append((low, high, mine, swap(mine)))
    bounds = bounds_of(width, SHARES)
    cuts = cut_rows(core, w_down, bounds)
    downs = []
    for cut in cuts:
        mine = go(cut, pair)
        downs.append((mine, swap(mine)))

    named = expert_ids[:, :, None] == jnp.arange(owners, dtype=jnp.int32)
    table = jnp.sum(jnp.where(named, route_weights[:, :, None], 0).astype(F32), axis=1)
    table = table.astype(BF16).T
    member = me // 2
    tables = table[None]
    for bit in range(members.bit_length() - 1):
        perm = [(i, i ^ (2 << bit)) for i in range(owners)]
        other = go(tables, perm)
        low = (member >> bit) % 2 == 0
        tables = jnp.where(low, jnp.concatenate([tables, other]), jnp.concatenate([other, tables]))
    order = ring_order(members)
    places = jnp.array([order.index(m) for m in range(members)], jnp.int32)
    offsets = [0]
    for step in range(1, full + 1):
        offsets += [-step, step]
    offsets.append(members // 2)
    place = places[member]
    sources = jnp.array(order, jnp.int32)[(place + jnp.array(offsets, jnp.int32)) % members]
    picked = jnp.take(tables, sources, axis=0).astype(F32)
    pick = jnp.arange(owners, dtype=jnp.int32)[None, :, None]
    weight_own = jnp.sum(jnp.where(pick == me, picked, 0), axis=1).reshape(-1, 1)
    weight_pair = jnp.sum(jnp.where(pick == (me ^ 1), picked, 0), axis=1).reshape(-1, 1)

    pair_scale = go(ia3_scale, pair)
    scales = []
    for low, high in pieces:
        both = [
            lax.dynamic_slice(pair_scale, (0, at + low), (1, high - low))
            for at in (first, half_units - first)
        ]
        scales.append(jnp.concatenate(both, axis=1))
    scale_pair = jnp.concatenate(scales, axis=1)

    token_blocks = gather(tokens)
    cotangent_blocks = gather(cotangent)
    early = 1 + 4 * EARLY
    count = rows * (1 + 2 * EARLY)
    total_rows = rows * members
    spans = (slice(0, count), slice(count, total_rows))
    everything = slice(0, units)

    def shape(height, size, dtype=F32):
        return jax.ShapeDtypeStruct((height, size), dtype)

    owns = []
    for n, group in enumerate((token_blocks[:early], token_blocks[early:])):
        height = spans[n].stop - spans[n].start
        (hidden,) = contract(
            group,
            [[([(w, width)], everything, 0)] for w in (w_gate, w_up)],
            False, [ia3_scale], [shape(height, units, BF16)], finish_own,
        )
        owns.append(hidden)

    pairs = []
    for piece, (low, high) in enumerate(pieces):
        size = high - low
        parts = []
        for start, stop, *arrays in projections:
            if low <= start < high:
                for side, array in enumerate(arrays):
                    for half in range(2):
                        take = slice(half * (stop - start), (half + 1) * (stop - start))
                        parts.append(([(array, width)], take, (2 * side + half) * size + start - low))
        (hidden,) = contract(
            token_blocks, [parts], False, [scales[piece]], [shape(total_rows, 2 * size, BF16)],
            finish_pair,
        )
        pairs.append(hidden)
    takes = [slice(low, high) for low, high in pieces]

    mixed = []
    for chunk, (low, high) in enumerate(bounds):
        *blocks, behind, ahead = both_out(
            owns, pairs, takes, w_down, *downs[chunk], (weight_own, weight_pair), low, split
        )
        ahead = go(ahead, forward)
        behind = go(behind, backward)
        for step in range(full, 0, -1):
            toward, back = hop_sum(blocks[2 * step], blocks[2 * step - 1], ahead, behind)
            ahead = go(toward, forward)
            behind = go(back, backward)
        mixed.append((blocks[0], ahead, behind))
    mixed = last_sum(mixed, rows, bounds)

    grad_own = 0.0
    early_back = 1 + 4 * EARLY_BACK
    middle = rows * (1 + 2 * EARLY_BACK)
    for n, (group, span) in enumerate(
        (
            (cotangent_blocks[:early_back], slice(0, middle)),
            (cotangent_blocks[early_back:], slice(middle, total_rows)),
        )
    ):
        hidden_rows = owns[0] if n == 0 else jnp.concatenate([owns[0][middle:], owns[1]])
        (grad,) = contract(
            group, [[([(w_down, width)], everything, 0)]], True,
            [weight_own[span], ia3_scale, hidden_rows], [shape(1, units)],
            functools.partial(finish_grad, slice(0, span.stop - span.start)),
        )
        grad_own += grad
    parts, place = [], 0
    for low, high in pieces:
        for side in range(2):
            segments = [(down[side], down[side].shape[1]) for down in downs]
            parts.append((segments, slice(low, high), place))
            place += high - low
    (grad_pair,) = contract(
        cotangent_blocks, [parts], True, [weight_pair, scale_pair, *pairs], [shape(1, units)],
        functools.partial(finish_grad, slice(None)),
    )
    sides, at = ([], []), 0
    for low, high in pieces:
        for side in range(2):
            sides[side].append(grad_pair[:, at : at + high - low])
            at += high - low
    mine, other = (jnp.concatenate(side, axis=1) for side in sides)
    halves = [jnp.concatenate(both, axis=1) for both in ((mine, other), (other, mine))]
    grad_pair = jnp.where(rep == 0, *halves)
    total = grad_own + go(grad_pair, pair)
    total = total + swap(total)
    return mixed, total


def exchanged(tokens, expert_ids, route_weights, cotangent, w_gate, w_up, w_down, ia3_scale):
    owners = lax.axis_size("exp")
    tok_rows, model_width = tokens.shape
    per_token = expert_ids.shape[1]
    capacity = tok_rows * per_token // owners + tok_rows * per_token // (8 * owners)
    flat_ids = expert_ids.reshape(-1)
    one_hot = (flat_ids[:, None] == jnp.arange(owners, dtype=jnp.int32)[None, :]).astype(jnp.int32)
    before = jnp.cumsum(one_hot, axis=0) - one_hot
    slot_index = jnp.sum(before * one_hot, axis=1)
    source_row = jnp.arange(tok_rows * per_token, dtype=jnp.int32) // per_token

    def into_slots(values):
        empty = jnp.zeros((owners, capacity) + values.shape[1:], values.dtype)
        return empty.at[flat_ids, slot_index].set(values)

    token_send = into_slots(tokens[source_row])
    weight_send = into_slots(route_weights.reshape(-1))
    token_recv, weight_recv = (
        lax.all_to_all(token_send, "exp", split_axis=0, concat_axis=0, tiled=True),
        lax.all_to_all(weight_send, "exp", split_axis=0, concat_axis=0, tiled=True),
    )
    received_rows = token_recv.reshape(-1, model_width)
    gate_pre = jnp.dot(received_rows, w_gate[0], preferred_element_type=jnp.float32)
    up_pre = jnp.dot(received_rows, w_up[0], preferred_element_type=jnp.float32)
    activated = jax.nn.silu(gate_pre) * up_pre
    hidden = (ia3_scale[0][None, :] * activated).astype(jnp.bfloat16)
    expert_out = jnp.dot(hidden, w_down[0], preferred_element_type=jnp.float32).astype(jnp.bfloat16)
    returned = lax.all_to_all(
        expert_out.reshape(owners, capacity, model_width),
        "exp",
        split_axis=0,
        concat_axis=0,
        tiled=True,
    )
    picked = returned[flat_ids, slot_index].reshape(tok_rows, per_token, model_width)
    mixed = jnp.einsum(
        "tkd,tk->td", picked, route_weights, preferred_element_type=jnp.float32
    ).astype(jnp.bfloat16)
    grad_send = into_slots(cotangent[source_row])
    grad_recv = lax.all_to_all(grad_send, "exp", split_axis=0, concat_axis=0, tiled=True)
    back_proj = lax.dot_general(
        grad_recv.reshape(-1, model_width),
        w_down[0],
        (((1,), (1,)), ((), ())),
        preferred_element_type=jnp.float32,
    )
    weight_rows = weight_recv.reshape(-1).astype(jnp.float32)
    local_grad = jnp.sum(weight_rows[:, None] * activated * back_proj, axis=0)
    summed = lax.psum(local_grad, "rep")
    return (mixed, summed[None, :])


def dense(owners, per_token):
    return owners in (16,) and 2 * per_token >= owners


def shards(*arrays):
    if not dense(lax.axis_size("exp"), arrays[1].shape[1]):
        return exchanged(*arrays)
    return gathered(*arrays)


def solution(mesh):
    in_specs = (
        P(("rep", "exp"), None),
        P(("rep", "exp"), None),
        P(("rep", "exp"), None),
        P(("rep", "exp"), None),
        P("exp", None, None),
        P("exp", None, None),
        P("exp", None, None),
        P("exp", None),
    )
    out_specs = (P(("rep", "exp"), None), P("exp", None))
    return jax.shard_map(shards, mesh=mesh, in_specs=in_specs, out_specs=out_specs, check_vma=False)
```

```python
import functools
import math

import jax
import jax.numpy as jnp
from jax import lax
from jax.experimental import pallas as pl
from jax.experimental.pallas import tpu as pltpu
from jax.sharding import PartitionSpec as P

TILES = (1, 1, 1)
PIECES = (2, 1)
SHARES = (3, 3, 2)
SLOTS = 3
LANES = 128
EARLY = 2
EARLY_BACK = 2
F32 = jnp.float32
BF16 = jnp.bfloat16
VMEM_LIMIT = 60 * 1024 * 1024
SMALL_LIMIT = 8 * 1024 * 1024


def ring_order(members):
    return list(range(0, members, 2)) + list(reversed(range(1, members, 2)))


def ring_perm(members, step):
    order = ring_order(members)
    perm = []
    for parity in range(2):
        for place, member in enumerate(order):
            target = order[(place + step) % members]
            perm.append((2 * member + parity, 2 * target + parity))
    return perm


def bounds_of(width, shares):
    edges = [0]
    for share in shares:
        edges.append(edges[-1] + width * share // sum(shares))
    return list(zip(edges[:-1], edges[1:]))


def whole(shape):
    return pl.BlockSpec(shape, lambda *_: (0,) * len(shape))


def params():
    return pltpu.CompilerParams(vmem_limit_bytes=VMEM_LIMIT)


def cost(flops, *arrays):
    moved = sum(math.prod(a.shape) * a.dtype.itemsize for a in arrays)
    return pl.CostEstimate(flops=flops, transcendentals=0, bytes_accessed=moved)


def cut_columns(core, w_gate, w_up, low, high):
    depth, units = w_gate.shape
    half, size = units // 2, high - low
    step = math.gcd(depth, 1024)
    steps = depth // step

    def body(core_ref, gate_ref, up_ref, out_ref, held, sems, out_sems):
        first = pl.multiple_of(core_ref[0] * half + low, LANES)
        ins, outs = [], []
        for i in range(steps):
            span = pl.ds(i * step, step)
            for n, ref in enumerate((gate_ref, up_ref)):
                source = ref.at[span, pl.ds(first, size)]
                ins.append(pltpu.make_async_copy(source, held.at[span, pl.ds(n * size, size)], sems.at[i, n]))
            outs.append(pltpu.make_async_copy(held.at[span, :], out_ref.at[span, :], out_sems.at[i]))
        for copy in ins:
            copy.start()
        for i in range(steps):
            ins[2 * i].wait()
            ins[2 * i + 1].wait()
            outs[i].start()
        for copy in outs:
            copy.wait()

    out = jax.ShapeDtypeStruct((depth, 2 * size), w_gate.dtype)
    return pl.pallas_call(
        body,
        out_shape=out,
        grid_spec=pltpu.PrefetchScalarGridSpec(
            num_scalar_prefetch=1,
            grid=(1,),
            in_specs=[pl.BlockSpec(memory_space=pltpu.HBM)] * 2,
            out_specs=pl.BlockSpec(memory_space=pltpu.HBM),
            scratch_shapes=[
                pltpu.VMEM(out.shape, out.dtype),
                pltpu.SemaphoreType.DMA((steps, 2)),
                pltpu.SemaphoreType.DMA((steps,)),
            ],
        ),
        compiler_params=params(),
        cost_estimate=cost(0, out, out),
        name="cut_columns",
    )(core, w_gate, w_up)


def cut_rows(core, w_down, bounds):
    half, width = w_down.shape[0] // 2, w_down.shape[1]
    count = len(bounds)

    def body(core_ref, in_ref, *refs):
        out_refs, (held, sems, out_sems) = refs[:count], refs[count:]
        rows = pl.ds(pl.multiple_of(core_ref[0] * half, half), half)
        ins, outs = [], []
        for n, (low, high) in enumerate(bounds):
            span = pl.ds(low, high - low)
            ins.append(pltpu.make_async_copy(in_ref.at[rows, span], held.at[:, span], sems.at[n]))
            outs.append(pltpu.make_async_copy(held.at[:, span], out_refs[n], out_sems.at[n]))
        for copy in ins:
            copy.start()
        for copy, out in zip(ins, outs):
            copy.wait()
            out.start()
        for out in outs:
            out.wait()

    outs = [jax.ShapeDtypeStruct((half, high - low), w_down.dtype) for low, high in bounds]
    return pl.pallas_call(
        body,
        out_shape=outs,
        grid_spec=pltpu.PrefetchScalarGridSpec(
            num_scalar_prefetch=1,
            grid=(1,),
            in_specs=[pl.BlockSpec(memory_space=pltpu.HBM)],
            out_specs=[pl.BlockSpec(memory_space=pltpu.HBM)] * count,
            scratch_shapes=[
                pltpu.VMEM((half, width), w_down.dtype),
                pltpu.SemaphoreType.DMA((count,)),
                pltpu.SemaphoreType.DMA((count,)),
            ],
        ),
        compiler_params=params(),
        cost_estimate=cost(0, *outs, *outs),
        name="cut_rows",
    )(core, w_down)


def contract(blocks, groups, transposed, extras, outs, finish):
    starts = [0]
    for block in blocks:
        starts.append(starts[-1] + block.shape[0])
    rows, width = starts[-1], blocks[0].shape[1]
    lengths = [length for parts in groups for segments, _, _ in parts for _, length in segments]
    step = math.gcd(1024, width, *lengths)
    arrays, copies_of, sizes = [], [], []
    for parts in groups:
        size = 0
        for segments, take, place in parts:
            at = 0
            for array, length in segments:
                if not any(array is other for other in arrays):
                    arrays.append(array)
                index = next(i for i, other in enumerate(arrays) if other is array)
                assert length % step == 0
                copies_of.append((len(sizes), index, at // step, length // step, take, place))
                at += length
            size = max(size, place + take.stop - take.start)
        sizes.append(size)
    steps = width // step
    count, parts_count = len(blocks), len(copies_of)
    slots = min(SLOTS, steps)

    def body(*refs):
        block_refs, refs = refs[:count], refs[count:]
        array_refs, refs = refs[: len(arrays)], refs[len(arrays) :]
        extra_refs, refs = refs[: len(extras)], refs[len(extras) :]
        out_refs, refs = refs[: len(outs)], refs[len(outs) :]
        held, sems, weight_sems, refs = refs[0], refs[1], refs[2], refs[3:]
        weight_refs, totals = refs[: len(sizes)], refs[len(sizes) :]
        k = pl.program_id(0)

        def block_copies(at, slot):
            columns = pl.ds(pl.multiple_of(at * step, step), step)
            return [
                pltpu.make_async_copy(
                    ref.at[:, columns],
                    held.at[slot, pl.ds(starts[i], blocks[i].shape[0]), :],
                    sems.at[slot, i],
                )
                for i, ref in enumerate(block_refs)
            ]

        def weight_copy(part, at, slot):
            j, index, first, _, take, place = copies_of[part]
            along = pl.ds(pl.multiple_of((at - first) * step, step), step)
            across = pl.ds(take.start, take.stop - take.start)
            there = pl.ds(place, take.stop - take.start)
            if transposed:
                source, target = array_refs[index].at[across, along], weight_refs[j].at[slot, there, :]
            else:
                source, target = array_refs[index].at[along, across], weight_refs[j].at[slot, :, there]
            return pltpu.make_async_copy(source, target, weight_sems.at[slot, part])

        def each(at, slot, do):
            for copy in block_copies(at, slot):
                do(copy)
            for part, (_, _, first, length, _, _) in enumerate(copies_of):
                if length == steps:
                    do(weight_copy(part, at, slot))
                else:

                    @pl.when((at >= first) & (at < first + length))
                    def _():
                        do(weight_copy(part, at, slot))

        slot = lax.rem(k, slots)

        @pl.when(k == 0)
        def _():
            for early in range(slots - 1):
                each(early, early, lambda copy: copy.start())

        @pl.when(k + slots - 1 < steps)
        def _():
            each(k + slots - 1, lax.rem(k + slots - 1, slots), lambda copy: copy.start())

        each(k, slot, lambda copy: copy.wait())
        dims = (((1,), (1 if transposed else 0,)), ((), ()))

        def product(j):
            return lax.dot_general(held[slot], weight_refs[j][slot], dims, preferred_element_type=F32)

        @pl.when(k == 0)
        def _():
            for j, total in enumerate(totals):
                total[...] = product(j)

        @pl.when(k > 0)
        def _():
            for j, total in enumerate(totals):
                total[...] += product(j)

        @pl.when(k == steps - 1)
        def _():
            finish(totals, extra_refs, out_refs)

    specs = [pl.BlockSpec(memory_space=pltpu.HBM)] * (count + len(arrays))
    specs += [pl.BlockSpec(a.shape, lambda k: (0, 0), pipeline_mode=pl.Buffered(1)) for a in extras]
    dtype = blocks[0].dtype
    return pl.pallas_call(
        body,
        out_shape=outs,
        grid=(steps,),
        in_specs=specs,
        out_specs=[whole(out.shape) for out in outs],
        scratch_shapes=[
            pltpu.VMEM((slots, rows, step), dtype),
            pltpu.SemaphoreType.DMA((slots, count)),
            pltpu.SemaphoreType.DMA((slots, parts_count)),
            *[pltpu.VMEM((slots, size, step) if transposed else (slots, step, size), dtype) for size in sizes],
            *[pltpu.VMEM((rows, size), F32) for size in sizes],
        ],
        compiler_params=params(),
        cost_estimate=cost(2 * rows * sum(sizes) * width, *outs),
    )(*blocks, *arrays, *extras)


def silu(v):
    return v / (1.0 + jnp.exp(-v))


def finish_own(totals, extra_refs, out_refs):
    act = silu(totals[0][...]) * totals[1][...]
    out_refs[0][...] = (extra_refs[0][...] * act).astype(BF16)


def finish_pair(totals, extra_refs, out_refs):
    total = totals[0]
    size = total.shape[1] // 4
    for side in range(2):
        gate, up = total[:, 2 * side * size : (2 * side + 1) * size], total[:, (2 * side + 1) * size : (2 * side + 2) * size]
        columns = slice(side * size, (side + 1) * size)
        out_refs[0][:, columns] = (extra_refs[0][:, columns] * (silu(gate) * up)).astype(BF16)


def finish_grad(span, totals, extra_refs, out_refs):
    weight, scale, hiddens = extra_refs[0], extra_refs[1], extra_refs[2:]
    first = 0
    for hidden in hiddens:
        columns = slice(first, first + hidden.shape[1])
        term = weight[...] * hidden[span, :].astype(F32) * totals[0][:, columns]
        out_refs[0][:, columns] = jnp.sum(term, axis=0, keepdims=True) / scale[:, columns]
        first += hidden.shape[1]


def both_out(owns, pairs, takes, w_down, mine, other, weights, low, split):
    rows = sum(own.shape[0] for own in owns)
    heights = [2 * split] * (rows // split // 2 - 1) + [split, split]
    units = w_down.shape[0]
    width = mine.shape[1]
    step = math.gcd(math.gcd(low, width), 512)

    def body(*refs):
        own_refs, refs = refs[: len(owns)], refs[len(owns) :]
        pair_refs, refs = refs[: len(pairs)], refs[len(pairs) :]
        w_ref, mine_ref, other_ref, weight_own, weight_pair, *out_refs, hidden = refs

        @pl.when(pl.program_id(0) == 0)
        def _():
            done = 0
            for ref in own_refs:
                hidden[0, done : done + ref.shape[0], :] = ref[...]
                done += ref.shape[0]
            done = 0
            for ref in pair_refs:
                hidden[1, :, done : done + ref.shape[1]] = ref[...]
                done += ref.shape[1]

        w = jnp.concatenate([ref[take, :] for take in takes for ref in (mine_ref, other_ref)], axis=0)
        total = weight_own[...] * jnp.dot(hidden[0], w_ref[...], preferred_element_type=F32)
        total += weight_pair[...] * jnp.dot(hidden[1], w, preferred_element_type=F32)
        total = total.astype(BF16)
        done = 0
        for out_ref in out_refs:
            out_ref[...] = total[done : done + out_ref.shape[0]]
            done += out_ref.shape[0]

    def columns(height, first=0):
        return pl.BlockSpec((height, step), lambda j: (0, first // step + j))

    def fixed(a):
        return pl.BlockSpec(a.shape, lambda j: (0, 0), pipeline_mode=pl.Buffered(1))

    outs = [jax.ShapeDtypeStruct((height, width), BF16) for height in heights]
    return pl.pallas_call(
        body,
        out_shape=outs,
        grid=(width // step,),
        in_specs=[fixed(a) for a in (*owns, *pairs)]
        + [columns(units, low), columns(mine.shape[0]), columns(mine.shape[0])]
        + [fixed(a) for a in weights],
        out_specs=[columns(height) for height in heights],
        scratch_shapes=[pltpu.VMEM((2, rows, units), BF16)],
        compiler_params=params(),
        cost_estimate=cost(4 * rows * units * width, *outs),
    )(*owns, *pairs, w_down, mine, other, *weights)


def hop_sum(near, far, ahead, behind):
    rows, width = near.shape
    split = ahead.shape[0]

    def body(near_ref, far_ref, ahead_ref, behind_ref, out_toward, out_back, toward, back, fore, aft, sems):
        sources = (near_ref, far_ref, ahead_ref, behind_ref)
        copies = [
            pltpu.make_async_copy(source, target, sems.at[i])
            for i, (source, target) in enumerate(zip(sources, (toward, back, fore, aft)))
        ]
        for copy in copies:
            copy.start()
        for copy in copies:
            copy.wait()
        low, high = (slice(None), slice(None)) if split == rows else (slice(0, split), slice(split, rows))
        if split != rows:
            out_toward[low, :] = toward[low, :]
            out_back[high, :] = back[high, :]
        out_toward[high, :] = (toward[high, :].astype(F32) + fore[...].astype(F32)).astype(BF16)
        out_back[low, :] = (back[low, :].astype(F32) + aft[...].astype(F32)).astype(BF16)

    out = jax.ShapeDtypeStruct((rows, width), BF16)
    return pl.pallas_call(
        body,
        out_shape=[out, out],
        grid=(1,),
        in_specs=[pl.BlockSpec(memory_space=pltpu.HBM)] * 4,
        out_specs=[whole(out.shape)] * 2,
        scratch_shapes=[
            pltpu.VMEM(out.shape, BF16),
            pltpu.VMEM(out.shape, BF16),
            pltpu.VMEM(ahead.shape, BF16),
            pltpu.VMEM(behind.shape, BF16),
            pltpu.SemaphoreType.DMA((4,)),
        ],
        compiler_params=pltpu.CompilerParams(vmem_limit_bytes=SMALL_LIMIT),
        cost_estimate=cost(0, out, out, out, out),
    )(near, far, ahead, behind)


def last_sum(chunks, rows, bounds):
    flat = [a for chunk in chunks for a in chunk]

    def body(*refs):
        out_ref, held, sems = refs[len(flat) :]
        copies = []
        for n, (low, high) in enumerate(bounds):
            for i, ref in enumerate(refs[3 * n : 3 * n + 3]):
                source = ref.at[pl.ds(0, rows), :]
                copies.append(pltpu.make_async_copy(source, held.at[i, :, pl.ds(low, high - low)], sems.at[n, i]))
        for copy in copies:
            copy.start()
        for copy in copies:
            copy.wait()
        total = held[0].astype(F32) + held[1].astype(F32) + held[2].astype(F32)
        out_ref[...] = total.astype(BF16)

    out = jax.ShapeDtypeStruct((rows, bounds[-1][1]), BF16)
    return pl.pallas_call(
        body,
        out_shape=out,
        grid=(1,),
        in_specs=[pl.BlockSpec(memory_space=pltpu.HBM)] * len(flat),
        out_specs=whole(out.shape),
        scratch_shapes=[
            pltpu.VMEM((3, *out.shape), BF16),
            pltpu.SemaphoreType.DMA((len(bounds), 3)),
        ],
        compiler_params=pltpu.CompilerParams(vmem_limit_bytes=SMALL_LIMIT),
        cost_estimate=cost(0, out, out, out, out),
    )(*flat)


def gathered(tokens, expert_ids, route_weights, cotangent, w_gate, w_up, w_down, ia3_scale):
    owners = lax.axis_size("exp")
    members = owners // 2
    rows, width = tokens.shape
    units = w_gate.shape[2]
    half_units = units // 2
    me = lax.axis_index("exp")
    rep = lax.axis_index("rep")
    w_gate, w_up, w_down = w_gate[0], w_up[0], w_down[0]
    forward, backward = ring_perm(members, 1), ring_perm(members, -1)
    pair = [(i, i ^ 1) for i in range(owners)]
    cores = [(0, 1), (1, 0)]
    full = members // 2 - 1
    split = rows // 2

    def go(value, perm):
        return lax.ppermute(value, "exp", perm)

    def swap(value):
        return lax.ppermute(value, "rep", cores)

    def gather(block):
        halves = (block[:split], block[split:])
        ahead, behind = list(halves), list(halves)
        blocks = [block]
        for _ in range(1, full + 1):
            ahead = [go(ahead[h], forward) for h in range(2)]
            behind = [go(behind[h], backward) for h in range(2)]
            blocks += ahead + behind
        blocks.append(go(ahead[0], forward))
        blocks.append(go(behind[1], backward))
        return blocks

    pieces = bounds_of(half_units, PIECES)
    first = rep * half_units
    core = jnp.full((1,), rep, jnp.int32)
    projections = []
    for low, high in bounds_of(half_units, TILES):
        cut = cut_columns(core, w_gate, w_up, low, high)
        mine = go(cut, pair)
        projections.append((low, high, mine, swap(mine)))
    bounds = bounds_of(width, SHARES)
    cuts = cut_rows(core, w_down, bounds)
    downs = []
    for cut in cuts:
        mine = go(cut, pair)
        downs.append((mine, swap(mine)))

    named = expert_ids[:, :, None] == jnp.arange(owners, dtype=jnp.int32)
    table = jnp.sum(jnp.where(named, route_weights[:, :, None], 0).astype(F32), axis=1)
    table = table.astype(BF16).T
    member = me // 2
    tables = table[None]
    for bit in range(members.bit_length() - 1):
        perm = [(i, i ^ (2 << bit)) for i in range(owners)]
        other = go(tables, perm)
        low = (member >> bit) % 2 == 0
        tables = jnp.where(low, jnp.concatenate([tables, other]), jnp.concatenate([other, tables]))
    order = ring_order(members)
    places = jnp.array([order.index(m) for m in range(members)], jnp.int32)
    offsets = [0]
    for step in range(1, full + 1):
        offsets += [-step, step]
    offsets.append(members // 2)
    place = places[member]
    sources = jnp.array(order, jnp.int32)[(place + jnp.array(offsets, jnp.int32)) % members]
    picked = jnp.take(tables, sources, axis=0).astype(F32)
    pick = jnp.arange(owners, dtype=jnp.int32)[None, :, None]
    weight_own = jnp.sum(jnp.where(pick == me, picked, 0), axis=1).reshape(-1, 1)
    weight_pair = jnp.sum(jnp.where(pick == (me ^ 1), picked, 0), axis=1).reshape(-1, 1)

    pair_scale = go(ia3_scale, pair)
    scales = []
    for low, high in pieces:
        both = [
            lax.dynamic_slice(pair_scale, (0, at + low), (1, high - low))
            for at in (first, half_units - first)
        ]
        scales.append(jnp.concatenate(both, axis=1))
    scale_pair = jnp.concatenate(scales, axis=1)

    token_blocks = gather(tokens)
    cotangent_blocks = gather(cotangent)
    early = 1 + 4 * EARLY
    count = rows * (1 + 2 * EARLY)
    total_rows = rows * members
    spans = (slice(0, count), slice(count, total_rows))
    everything = slice(0, units)

    def shape(height, size, dtype=F32):
        return jax.ShapeDtypeStruct((height, size), dtype)

    owns = []
    for n, group in enumerate((token_blocks[:early], token_blocks[early:])):
        height = spans[n].stop - spans[n].start
        (hidden,) = contract(
            group,
            [[([(w, width)], everything, 0)] for w in (w_gate, w_up)],
            False, [ia3_scale], [shape(height, units, BF16)], finish_own,
        )
        owns.append(hidden)

    pairs = []
    for piece, (low, high) in enumerate(pieces):
        size = high - low
        parts = []
        for start, stop, *arrays in projections:
            if low <= start < high:
                for side, array in enumerate(arrays):
                    for half in range(2):
                        take = slice(half * (stop - start), (half + 1) * (stop - start))
                        parts.append(([(array, width)], take, (2 * side + half) * size + start - low))
        (hidden,) = contract(
            token_blocks, [parts], False, [scales[piece]], [shape(total_rows, 2 * size, BF16)],
            finish_pair,
        )
        pairs.append(hidden)
    takes = [slice(low, high) for low, high in pieces]

    mixed = []
    for chunk, (low, high) in enumerate(bounds):
        *blocks, behind, ahead = both_out(
            owns, pairs, takes, w_down, *downs[chunk], (weight_own, weight_pair), low, split
        )
        ahead = go(ahead, forward)
        behind = go(behind, backward)
        for step in range(full, 0, -1):
            toward, back = hop_sum(blocks[2 * step], blocks[2 * step - 1], ahead, behind)
            ahead = go(toward, forward)
            behind = go(back, backward)
        mixed.append((blocks[0], ahead, behind))
    mixed = last_sum(mixed, rows, bounds)

    grad_own = 0.0
    early_back = 1 + 4 * EARLY_BACK
    middle = rows * (1 + 2 * EARLY_BACK)
    for n, (group, span) in enumerate(
        (
            (cotangent_blocks[:early_back], slice(0, middle)),
            (cotangent_blocks[early_back:], slice(middle, total_rows)),
        )
    ):
        hidden_rows = owns[0] if n == 0 else jnp.concatenate([owns[0][middle:], owns[1]])
        (grad,) = contract(
            group, [[([(w_down, width)], everything, 0)]], True,
            [weight_own[span], ia3_scale, hidden_rows], [shape(1, units)],
            functools.partial(finish_grad, slice(0, span.stop - span.start)),
        )
        grad_own += grad
    parts, place = [], 0
    for low, high in pieces:
        for side in range(2):
            segments = [(down[side], down[side].shape[1]) for down in downs]
            parts.append((segments, slice(low, high), place))
            place += high - low
    (grad_pair,) = contract(
        cotangent_blocks, [parts], True, [weight_pair, scale_pair, *pairs], [shape(1, units)],
        functools.partial(finish_grad, slice(None)),
    )
    sides, at = ([], []), 0
    for low, high in pieces:
        for side in range(2):
            sides[side].append(grad_pair[:, at : at + high - low])
            at += high - low
    mine, other = (jnp.concatenate(side, axis=1) for side in sides)
    halves = [jnp.concatenate(both, axis=1) for both in ((mine, other), (other, mine))]
    grad_pair = jnp.where(rep == 0, *halves)
    total = grad_own + go(grad_pair, pair)
    total = total + swap(total)
    return mixed, total


def exchanged(tokens, expert_ids, route_weights, cotangent, w_gate, w_up, w_down, ia3_scale):
    owners = lax.axis_size("exp")
    tok_rows, model_width = tokens.shape
    per_token = expert_ids.shape[1]
    capacity = tok_rows * per_token // owners + tok_rows * per_token // (8 * owners)
    flat_ids = expert_ids.reshape(-1)
    one_hot = (flat_ids[:, None] == jnp.arange(owners, dtype=jnp.int32)[None, :]).astype(jnp.int32)
    before = jnp.cumsum(one_hot, axis=0) - one_hot
    slot_index = jnp.sum(before * one_hot, axis=1)
    source_row = jnp.arange(tok_rows * per_token, dtype=jnp.int32) // per_token

    def into_slots(values):
        empty = jnp.zeros((owners, capacity) + values.shape[1:], values.dtype)
        return empty.at[flat_ids, slot_index].set(values)

    token_send = into_slots(tokens[source_row])
    weight_send = into_slots(route_weights.reshape(-1))
    token_recv, weight_recv = (
        lax.all_to_all(token_send, "exp", split_axis=0, concat_axis=0, tiled=True),
        lax.all_to_all(weight_send, "exp", split_axis=0, concat_axis=0, tiled=True),
    )
    received_rows = token_recv.reshape(-1, model_width)
    gate_pre = jnp.dot(received_rows, w_gate[0], preferred_element_type=jnp.float32)
    up_pre = jnp.dot(received_rows, w_up[0], preferred_element_type=jnp.float32)
    activated = jax.nn.silu(gate_pre) * up_pre
    hidden = (ia3_scale[0][None, :] * activated).astype(jnp.bfloat16)
    expert_out = jnp.dot(hidden, w_down[0], preferred_element_type=jnp.float32).astype(jnp.bfloat16)
    returned = lax.all_to_all(
        expert_out.reshape(owners, capacity, model_width),
        "exp",
        split_axis=0,
        concat_axis=0,
        tiled=True,
    )
    picked = returned[flat_ids, slot_index].reshape(tok_rows, per_token, model_width)
    mixed = jnp.einsum(
        "tkd,tk->td", picked, route_weights, preferred_element_type=jnp.float32
    ).astype(jnp.bfloat16)
    grad_send = into_slots(cotangent[source_row])
    grad_recv = lax.all_to_all(grad_send, "exp", split_axis=0, concat_axis=0, tiled=True)
    back_proj = lax.dot_general(
        grad_recv.reshape(-1, model_width),
        w_down[0],
        (((1,), (1,)), ((), ())),
        preferred_element_type=jnp.float32,
    )
    weight_rows = weight_recv.reshape(-1).astype(jnp.float32)
    local_grad = jnp.sum(weight_rows[:, None] * activated * back_proj, axis=0)
    summed = lax.psum(local_grad, "rep")
    return (mixed, summed[None, :])


def dense(owners, per_token):
    return owners in (16,) and 2 * per_token >= owners


def shards(*arrays):
    if not dense(lax.axis_size("exp"), arrays[1].shape[1]):
        return exchanged(*arrays)
    return gathered(*arrays)


def solution(mesh):
    in_specs = (
        P(("rep", "exp"), None),
        P(("rep", "exp"), None),
        P(("rep", "exp"), None),
        P(("rep", "exp"), None),
        P("exp", None, None),
        P("exp", None, None),
        P("exp", None, None),
        P("exp", None),
    )
    out_specs = (P(("rep", "exp"), None), P("exp", None))
    return jax.shard_map(shards, mesh=mesh, in_specs=in_specs, out_specs=out_specs, check_vma=False)
```
